128 devices in a mesh: dp: 4 (over y), context: 4 (over z), tensor: 8 (over x, core).
Axes of the slice: x: 4, y: 4, z: 4, core: 2. Of those that a mesh axis runs over, the one named last changes fastest.
Arguments:
- panels: bfloat16 [4, 4, 65, 32, 512], P('dp', 'context', None, None, 'tensor'), may hold values from -6 to 6
- lengths: int32 [4, 4], P('dp'), may hold values from 1 to 65, as said below
- segments: int32 [4, 4096], P('dp', ('context', 'tensor')), may hold values from 0 to 7, never falling along the last dimension, each value on 1 to 1024 neighbouring positions
- front_weight: bfloat16 [512, 1536], P('tensor'), may hold values from -0.25 to 0.25
- conv_kernel: float32 [5, 1536], replicated, may hold values from -2 to 2
- gain: float32 [1536], replicated, may hold values from 0.25 to 1.75
- up_weight: bfloat16 [1536, 6144], P(None, 'tensor'), may hold values from -0.15625 to 0.15625
- down_weight: bfloat16 [6144, 1536], P('tensor'), may hold values from -0.078125 to 0.078125
- cotangent: bfloat16 [4, 4096, 1536], P('dp', ('context', 'tensor')), may hold values from -0.1875 to 0.1875
Outputs:
- grad_front: float32 [512, 1536], P('tensor')
- grad_kernel: float32 [5, 1536], replicated
- grad_gain: float32 [1536], replicated
- grad_up: float32 [1536, 6144], P(None, 'tensor')
- grad_down: float32 [6144, 1536], P('tensor')
The draws below stay inside these ranges and needn't reach their ends.
Inputs may be any that keep to these rules, and one draw needn't show every extreme that they name: `lengths`: each stream's counts sum to 128; in every stream one loader shard, which one varies, holds exactly 65 panels and every other shard one or more; slots past a shard's count are not used. `segments`: document numbers never fall along a stream; each document spans 1 to 1024 frames.
All inputs are finite; a program needn't handle non-finite values.
Results may differ from the reference program's by a relative error of at most 0.007.
Values may be sent and summed in bfloat16 or wider, within the bound.
No kernel may reach another device: no remote copies, remote signals or barrier semaphores. Data moves between devices by JAX's collectives and lax.ppermute only.
A program may use at most 128 MiB of HBM per device.

```python
import math
import jax
import jax.numpy as jnp
import numpy as np
from jax import lax

D = 1536
FF = 6144
KER = 5
PANEL = 32
FEAT = 512
ROWS_OWN = 1024
PANELS_OWN = 32
PANELS_ALL = 128
SLOTS = 65
SEQ = 4096
STREAMS = 4
OWNERS = 4


def draw_lengths(key, part):

    def one_stream(stream_key):
        cut_key, order_key = jax.random.split(stream_key)
        cuts = jax.random.permutation(cut_key, 2 * PANELS_OWN - 2)[:2] + 1
        lower = jnp.minimum(cuts[0], cuts[1])
        upper = jnp.maximum(cuts[0], cuts[1])
        counts = jnp.stack([lower, upper - lower, 2 * PANELS_OWN - 1 - upper, jnp.full((), SLOTS, jnp.int32)]).astype(jnp.int32)
        order = jax.random.permutation(order_key, OWNERS)
        return counts[order].astype(jnp.int32)
    stream_keys = jax.random.split(jax.random.fold_in(key, 17), STREAMS)
    return jax.vmap(one_stream)(stream_keys)


def levels(key, extent, pieces, low, top_value):
    def one(position, blocks):
        draws = jax.random.uniform(jax.random.fold_in(jax.random.fold_in(key, 6), position), (blocks,), jnp.float32, low / len(pieces), top_value / len(pieces))
        return jnp.repeat(jnp.exp(draws), extent[position] // blocks).reshape((-1,) + (1,) * (len(extent) - position - 1))

    level = one(*pieces[0])
    for cut in pieces[1:]:
        level = level * one(*cut)
    return level


def profile(amount, total, reach, lean):
    portions = [(1 << 20) // math.isqrt(rank ** lean) + 1 for rank in range(2, amount + 1)]
    surplus, given = total - reach - (amount - 1), [1] * (amount - 1)
    while surplus > 0:
        movable = [i for i in range(amount - 1) if given[i] < reach]
        whole, left = sum([portions[i] for i in movable]), surplus
        for i in movable:
            extra = min(reach - given[i], max(1, left * portions[i] // whole), surplus)
            given[i] = given[i] + extra
            surplus = surplus - extra
    return np.array([reach] + given)


def uneven_parts(own_key, number_of, total, bound, lean):
    if number_of == 2:
        one = jax.random.randint(own_key, (), max(1, total - bound), min(bound, total - 1) + 1)
        return jnp.stack([one, total - one])
    tallies = jnp.asarray(profile(number_of, total, bound, lean), jnp.int32)
    twos = (number_of - 1) // 2
    donor, taker = tallies[1:1 + 2 * twos:2], tallies[2:2 + 2 * twos:2]
    slack = jnp.minimum(donor - 1, bound - taker)
    moved = jax.random.randint(jax.random.fold_in(own_key, 1), (twos,), 0, 1 << 20) % (slack + 1)
    tallies = tallies.at[1:1 + 2 * twos:2].set(donor - moved).at[2:2 + 2 * twos:2].set(taker + moved)
    return tallies[jax.random.permutation(jax.random.fold_in(own_key, 2), number_of)]


def noise(key, shape, spread, most, pieces=(), kind=jnp.bfloat16):
    array = jax.random.normal(key, shape, jnp.float32) * spread
    if len(pieces) > 0:
        array = levels(key, shape, pieces, -0.22, 0.18) * array
    return jnp.clip(array, min=-most, max=most).astype(kind)


def setup_inputs(seed: int = 0) -> dict:
    key_list = jax.random.split(jax.random.key(seed), 10)
    return {
        "panels": noise(key_list[0], (STREAMS, OWNERS, SLOTS, PANEL, FEAT), 1.0, 6.0, ((0, 4), (1, 4), (4, 8))),
        "lengths": draw_lengths(jax.random.fold_in(key_list[9], 71), 0),
        "segments": jax.vmap(lambda own: jnp.searchsorted(jnp.cumsum(uneven_parts(own, 2 * OWNERS, SEQ, ROWS_OWN, 1)), jnp.arange(SEQ), side="right"))(jax.random.split(key_list[2], STREAMS)).reshape((STREAMS, SEQ)).astype(jnp.int32),
        "front_weight": noise(key_list[3], (FEAT, D), FEAT ** -0.5, 0.25, ((0, 8),)),
        "conv_kernel": noise(key_list[4], (KER, D), 0.4, 2.0, (), jnp.float32),
        "gain": jnp.clip(1.0 + 0.15 * jax.random.normal(key_list[5], (D,), jnp.float32), 0.25, 1.75),
        "up_weight": noise(key_list[6], (D, FF), D ** -0.5, 0.15625, ((1, 8),)),
        "down_weight": noise(key_list[7], (FF, D), FF ** -0.5, 0.078125, ((0, 8),)),
        "cotangent": noise(key_list[8], (STREAMS, SEQ, D), (4.0 / (STREAMS * SEQ) ** 0.5), 0.1875, ((0, 4), (1, 32))),
    }


def reference(panels, lengths, segments, front_weight, conv_kernel, gain, up_weight, down_weight, cotangent):
    grad_front = jnp.zeros((FEAT, D), jnp.float32)
    grad_kernel = jnp.zeros((KER, D), jnp.float32)
    grad_gain = jnp.zeros((D,), jnp.float32)
    grad_up = jnp.zeros((D, FF), jnp.float32)
    grad_down = jnp.zeros((FF, D), jnp.float32)
    for stream in range(STREAMS):
        counts = lengths[stream]
        starts = jnp.cumsum(counts) - counts
        wanted = jnp.arange(PANELS_ALL, dtype=jnp.int32)
        source = lax.optimization_barrier(jnp.sum((starts[None, :] <= wanted[:, None]).astype(jnp.int32), axis=1)) - 1
        slot = (wanted - starts[source]).astype(jnp.int32)
        stacked = panels[stream][source, slot].reshape(SEQ, FEAT)
        frames = jnp.dot(stacked, front_weight, preferred_element_type=jnp.float32).astype(jnp.bfloat16)
        seg = segments[stream]
        seg_pad = jnp.pad(seg, 2, constant_values=-1)
        same = [(seg_pad[j:j + SEQ] == seg).astype(jnp.float32)[:, None] for j in range(KER)]
        frames_wide = frames.astype(jnp.float32)
        frame_pad = jnp.pad(frames_wide, ((2, 2), (0, 0)))
        mixed = frames_wide
        for j in range(KER):
            mixed = mixed + conv_kernel[j] * same[j] * frame_pad[j:j + SEQ]
        center = mixed - lax.optimization_barrier(jnp.mean(mixed, axis=1, keepdims=True))
        rstd = lax.rsqrt(lax.optimization_barrier(jnp.mean(center * center, axis=1, keepdims=True)) + 1e-05)
        normed = center * rstd
        ln_out = (normed * gain).astype(jnp.bfloat16)
        pre = jnp.dot(ln_out, up_weight, preferred_element_type=jnp.float32)
        sig = jax.nn.sigmoid(pre)
        hidden = (pre * sig).astype(jnp.bfloat16)
        grad_out = cotangent[stream]
        grad_down = grad_down + 0.5 * jnp.dot(hidden.T, grad_out, preferred_element_type=jnp.float32)
        dhid = jnp.dot(grad_out, down_weight.T, preferred_element_type=jnp.float32)
        dpre = (0.5 * dhid * sig * (1.0 + pre * (1.0 - sig))).astype(jnp.bfloat16)
        grad_up = grad_up + jnp.dot(ln_out.T, dpre, preferred_element_type=jnp.float32)
        dln = jnp.dot(dpre, up_weight.T, preferred_element_type=jnp.float32)
        grad_gain = grad_gain + lax.optimization_barrier(jnp.sum(dln * normed, axis=0))
        dnorm = dln * gain
        dmixed = grad_out.astype(jnp.float32) + rstd * (dnorm - lax.optimization_barrier(jnp.mean(dnorm, axis=1, keepdims=True)) - normed * lax.optimization_barrier(jnp.mean(dnorm * normed, axis=1, keepdims=True)))
        dmixed = dmixed.astype(jnp.bfloat16)
        dwide = dmixed.astype(jnp.float32)
        grad_pad = jnp.pad(dwide, ((2, 2), (0, 0)))
        kernel_rows = [lax.optimization_barrier(jnp.sum(dwide * same[j] * frame_pad[j:j + SEQ], axis=0)) for j in range(KER)]
        grad_kernel = grad_kernel + jnp.stack(kernel_rows)
        dframes = dwide
        for j in range(KER):
            dframes = dframes + conv_kernel[j] * same[4 - j] * grad_pad[4 - j:4 - j + SEQ]
        dframes = dframes.astype(jnp.bfloat16)
        grad_front = grad_front + jnp.dot(stacked.T, dframes, preferred_element_type=jnp.float32)
    return (grad_front, grad_kernel, grad_gain, grad_up, grad_down)
```

```python
import functools

import jax
import jax.numpy as jnp
from jax import lax
from jax.experimental import pallas as pl
from jax.experimental.pallas import tpu as pltpu
from jax.sharding import PartitionSpec as P

BF = jnp.bfloat16
F32 = jnp.float32
ORDER = (0, 2, 6, 4)
XOR3 = (1, 3, 2)
UNIT = 16
HALO = 16


def vmem(limit):
    return pltpu.CompilerParams(vmem_limit_bytes=limit << 20)


def cost(flops, nbytes, trans=0):
    return pl.CostEstimate(flops=flops, bytes_accessed=nbytes, transcendentals=trans)


def full(shape):
    return pl.BlockSpec(shape, lambda *_: (0,) * len(shape))


def xor_send(value, axis, mask, size):
    return lax.ppermute(value, axis, [(i, i ^ mask) for i in range(size)])


def select_kernel(scal, panel_ref, seg_ref, *outs):
    owner, start, count = scal[0], scal[1], scal[2]
    rows = 40
    slots = panel_ref.shape[2]
    q = lax.broadcasted_iota(jnp.int32, (rows, slots), 0)
    slot = lax.broadcasted_iota(jnp.int32, (rows, slots), 1)
    picks = []
    for e in range(4):
        base = 32 * (owner ^ e)
        wanted = jnp.where(q < 32, base + q, jnp.where(q == 32, base - 1, base + 32))
        inside = (q < 34) & (wanted >= 0) & (wanted < 128)
        local = wanted - start
        hit = inside & (local == slot) & (slot < count)
        picks.append(hit.astype(F32).astype(BF))
    pick = jnp.concatenate(picks, axis=0)
    scratch = outs[4]
    for i in range(UNIT):
        pair = jnp.concatenate([panel_ref[i], panel_ref[i + UNIT]], axis=0)
        got = lax.dot_general(
            pick, pair, (((1,), (1,)), ((), ())), preferred_element_type=F32
        )
        scratch[pl.ds(i, 4 * rows, stride=UNIT), :] = got
    seg_row = seg_ref[...].astype(F32) + 1.0
    for e in range(4):
        target = owner ^ e
        base = e * rows * UNIT
        if e == 0:
            scratch[pl.ds(base + 34 * UNIT, 1), :] = seg_row
        else:
            up = (target == owner + 1).astype(F32)
            down = (target == owner - 1).astype(F32)
            scratch[pl.ds(base + 35 * UNIT, 1), :] = seg_row * up
            scratch[pl.ds(base + 36 * UNIT, 1), :] = seg_row * down
    for e in range(4):
        outs[e][...] = scratch[pl.ds(e * rows * UNIT, rows * UNIT), :].astype(BF)


def select_panels(scal, panels_t, seg):
    return pl.pallas_call(
        select_kernel,
        out_shape=[jax.ShapeDtypeStruct((640, 128), BF)] * 4,
        in_specs=[
            pl.BlockSpec(memory_space=pltpu.SMEM),
            full(panels_t.shape),
            full(seg.shape),
        ],
        out_specs=[full((640, 128))] * 4,
        grid=(1,),
        scratch_shapes=[pltpu.VMEM((2560, 128), F32)],
        compiler_params=vmem(24),
        cost_estimate=cost(2 * 160 * 65 * 2048, 2 << 20),
    )(scal, panels_t, seg)


def norm_kernel(
    order, a_ref, b_ref, wa_ref, wb_ref, kern_ref, gain_ref,
    ln_ref, normed_ref, rstd_ref, frames_ref, segs_ref, stack_ref,
    units, weight, segs, wide, near_segs,
):
    step = pl.program_id(0)

    @pl.when(step == 0)
    def _():
        lane = lax.broadcasted_iota(jnp.int32, (256, 256), 0)
        out_lane = lax.broadcasted_iota(jnp.int32, (256, 256), 1)
        source = (out_lane // 64 % 2) * 128 + (out_lane // 128) * 64 + out_lane % 64
        swap = (lane == source).astype(F32).astype(BF)
        for d in range(4):
            weight[pl.ds(128 * d, 64), :] = wa_ref[d]
            weight[pl.ds(128 * d + 64, 64), :] = wb_ref[d]
            both = jnp.concatenate([a_ref[d, pl.ds(0, 544), :], b_ref[d, pl.ds(0, 544), :]], axis=1)
            mixed = jnp.dot(both, swap, preferred_element_type=F32).astype(BF)
            for p in range(34):
                at = p + 1 if p < 32 else (0 if p == 32 else 33)
                for half in range(2):
                    units[2 * at + half, :, pl.ds(128 * d, 128)] = mixed[
                        16 * p : 16 * p + 16, 128 * half : 128 * half + 128
                    ]
        eye = (
            lax.broadcasted_iota(jnp.int32, (128, 128), 0)
            == lax.broadcasted_iota(jnp.int32, (128, 128), 1)
        ).astype(F32)
        ones = jnp.ones((128, 128), BF)

        def column(ref, d, q):
            row = ref[d, pl.ds(q * UNIT, 16), :].astype(F32)[0:1]
            return jnp.dot((eye * row).astype(BF), ones, preferred_element_type=F32)

        for c in range(2):
            ref = (a_ref, b_ref)[c]
            for d in range(4):
                at = order[4 * c + d]
                segs[pl.ds(pl.multiple_of(HALO + 128 * at, 16), 128), :] = column(ref, d, 34)

                @pl.when(at == 7)
                def _():
                    segs[pl.ds(0, HALO), :] = column(ref, d, 35)[128 - HALO :]

                @pl.when(at == 0)
                def _():
                    segs[pl.ds(HALO + 1024, HALO), :] = column(ref, d, 36)[:HALO]

    block = order[step]
    unit0 = 8 * block + 1
    rows = units[pl.ds(unit0, 10)].reshape(160, 512)
    frames = jnp.dot(rows, weight[...], preferred_element_type=F32)
    wide[...] = frames.astype(BF).astype(F32)

    @pl.when(step == 0)
    def _():
        stack_ref[...] = rows
        frames_ref[...] = wide[...]
        segs_ref[...] = segs[pl.ds(pl.multiple_of(128 * block, 128), 160), :]

    taps = [kern_ref[pl.ds(j, 1), :] for j in range(5)]
    gain = gain_ref[...]
    near_segs[...] = segs[pl.ds(pl.multiple_of(128 * block, 128), 160), :]

    for r in range(0, 128, 16):
        here = near_segs[pl.ds(HALO + r, 16), :]
        mixed = (1.0 + taps[2]) * wide[pl.ds(HALO + r, 16), :]
        for j in (0, 1, 3, 4):
            same = (near_segs[pl.ds(HALO - 2 + r + j, 16), :] == here).astype(F32)
            same = jnp.concatenate([same] * 12, axis=1)
            mixed = mixed + taps[j] * (same * wide[pl.ds(HALO - 2 + r + j, 16), :])
        mean = jnp.mean(mixed, axis=1, keepdims=True)
        center = mixed - mean
        rstd = lax.rsqrt(jnp.mean(center * center, axis=1, keepdims=True) + 1e-05)
        normed = center * rstd
        ln_ref[pl.ds(r, 16), :] = (normed * gain).astype(BF)

        @pl.when(step == 0)
        def _():
            normed_ref[pl.ds(r, 16), :] = normed
            rstd_ref[pl.ds(r, 16), :] = jnp.broadcast_to(rstd, (16, 128))


def normalise(order, a, b, wa, wb, kern, gain):
    d_model = kern.shape[1]
    return pl.pallas_call(
        norm_kernel,
        grid_spec=pltpu.PrefetchScalarGridSpec(
            num_scalar_prefetch=1,
            grid=(8,),
            in_specs=[
                full(a.shape), full(b.shape), full(wa.shape), full(wb.shape),
                full(kern.shape), full(gain.shape),
            ],
            out_specs=[
                pl.BlockSpec((128, d_model), lambda i, o: (i, 0)),
                full((128, d_model)), full((128, 128)), full((160, d_model)),
                full((160, 128)), full((160, 512)),
            ],
            scratch_shapes=[
                pltpu.VMEM((68, 16, 512), BF),
                pltpu.VMEM((512, d_model), BF),
                pltpu.VMEM((1056, 128), F32),
                pltpu.VMEM((160, d_model), F32),
                pltpu.VMEM((160, 128), F32),
            ],
        ),
        out_shape=[
            jax.ShapeDtypeStruct((1024, d_model), BF),
            jax.ShapeDtypeStruct((128, d_model), F32),
            jax.ShapeDtypeStruct((128, 128), F32),
            jax.ShapeDtypeStruct((160, d_model), F32),
            jax.ShapeDtypeStruct((160, 128), F32),
            jax.ShapeDtypeStruct((160, 512), BF),
        ],
        compiler_params=vmem(40),
        cost_estimate=cost(2 * 1280 * 512 * 1536, 10 << 20),
    )(order, a, b, wa, wb, kern, gain)


def ffn_kernel(ln_ref, ca_ref, cb_ref, up_ref, down_ref, hid_ref, dpre_ref, dln_ref, cot, sem):
    step = pl.program_id(0)

    @pl.when(step == 0)
    def _():
        pltpu.make_async_copy(ca_ref, cot.at[0], sem.at[0]).start()
        pltpu.make_async_copy(cb_ref, cot.at[1], sem.at[1]).start()

    pre = jnp.dot(ln_ref[...], up_ref[...], preferred_element_type=F32)

    @pl.when(step == 0)
    def _():
        pltpu.make_async_copy(ca_ref, cot.at[0], sem.at[0]).wait()

    @pl.when(step == 1)
    def _():
        pltpu.make_async_copy(cb_ref, cot.at[1], sem.at[1]).wait()

    dhid = lax.dot_general(
        cot[step], down_ref[...], (((1,), (1,)), ((), ())), preferred_element_type=F32
    )
    sig = 1.0 / (1.0 + jnp.exp(-pre))
    hid_ref[...] = (pre * sig).astype(BF)
    dpre = (0.5 * dhid * sig * (1.0 + pre * (1.0 - sig))).astype(BF)
    dpre_ref[...] = dpre
    dln_ref[0] = lax.dot_general(
        dpre, up_ref[...], (((1,), (1,)), ((), ())), preferred_element_type=F32
    ).astype(BF)


def feed_forward(ln, ca, cb, up, down):
    rows, d_model = ln.shape
    ff = up.shape[1]
    half = rows // 2
    return pl.pallas_call(
        ffn_kernel,
        grid=(2,),
        in_specs=[
            pl.BlockSpec((half, d_model), lambda i: (i, 0)),
            pl.BlockSpec(memory_space=pl.ANY),
            pl.BlockSpec(memory_space=pl.ANY),
            full(up.shape), full(down.shape),
        ],
        out_specs=[
            pl.BlockSpec((half, ff), lambda i: (i, 0)),
            pl.BlockSpec((half, ff), lambda i: (i, 0)),
            pl.BlockSpec((1, half, d_model), lambda i: (i, 0, 0)),
        ],
        out_shape=[
            jax.ShapeDtypeStruct((rows, ff), BF),
            jax.ShapeDtypeStruct((rows, ff), BF),
            jax.ShapeDtypeStruct((2, half, d_model), BF),
        ],
        scratch_shapes=[pltpu.VMEM((2, half, d_model), BF), pltpu.SemaphoreType.DMA((2,))],
        compiler_params=vmem(48),
        cost_estimate=cost(6 * rows * d_model * ff, 24 << 20, rows * ff),
    )(ln, ca, cb, up, down)


def piece_code(pos, r, k):
    ry, rz = pos[0] ^ (r // 4), pos[1] ^ (r % 4)
    code = (
        (((ry & 1) ^ (ry >> 1)) << 3) | (((rz & 1) ^ (rz >> 1)) << 2) | ((ry >> 1) << 1) | (rz >> 1)
    )
    return ((code << k) | (code >> (4 - k))) & 15


def weight_kernel(k, pos, hid_ref, ca_ref, cb_ref, ln_ref, dpre_ref, keep_ref, send_ref, both):
    half = ca_ref.shape[0]
    rows = (((0,), (0,)), ((), ()))
    down = lax.dot_general(hid_ref[pl.ds(0, half), :], ca_ref[...], rows, preferred_element_type=F32)
    down += lax.dot_general(hid_ref[pl.ds(half, half), :], cb_ref[...], rows, preferred_element_type=F32)
    down = (0.5 * down).astype(BF)
    up = lax.dot_general(ln_ref[...], dpre_ref[...], rows, preferred_element_type=F32).astype(BF)
    for r in range(16):
        code = piece_code(pos, r, k)
        both[code, pl.ds(0, 48), :] = down[48 * r : 48 * r + 48]
        both[code, pl.ds(48, 48), :] = up[48 * r : 48 * r + 48]
    keep_ref[...] = both[pl.ds(0, 8)]
    send_ref[...] = both[pl.ds(8, 8)]


def weight_part(k, pos, hidden, ca, cb, ln, dpre):
    rows = hidden.shape[0]
    half = rows // 2
    return pl.pallas_call(
        functools.partial(weight_kernel, k),
        grid=(1,),
        in_specs=[
            pl.BlockSpec(memory_space=pltpu.SMEM),
            full((rows, 768)),
            pl.BlockSpec((half, 384), lambda i: (0, k)),
            pl.BlockSpec((half, 384), lambda i: (0, k)),
            pl.BlockSpec((rows, 768), lambda i: (0, k // 2)),
            pl.BlockSpec((rows, 384), lambda i: (0, k % 2)),
        ],
        out_specs=[full((8, 96, 384))] * 2,
        out_shape=[jax.ShapeDtypeStruct((8, 96, 384), BF)] * 2,
        scratch_shapes=[pltpu.VMEM((16, 96, 384), BF)],
        compiler_params=vmem(32),
        cost_estimate=cost(4 * rows * 768 * 384, 7 << 20),
    )(pos, hidden, ca, cb, ln, dpre)


def place_kernel(pos, *refs):
    ins, (down_ref, up_ref) = refs[:8], refs[8:]
    for k in range(4):

        @pl.when(pl.program_id(0) == k)
        def _():
            cur, rec = ins[2 * k], ins[2 * k + 1]
            for r in range(16):
                code = piece_code(pos, r, k)

                @pl.when(code < 8)
                def _():
                    down_ref[pl.ds(48 * r, 48), :] = cur[code, pl.ds(0, 48), :].astype(F32)
                    up_ref[pl.ds(48 * r, 48), :] = cur[code, pl.ds(48, 48), :].astype(F32)

                @pl.when(code >= 8)
                def _():
                    down_ref[pl.ds(48 * r, 48), :] = rec[code - 8, pl.ds(0, 48), :].astype(F32)
                    up_ref[pl.ds(48 * r, 48), :] = rec[code - 8, pl.ds(48, 48), :].astype(F32)


def place(pos, pieces):
    return pl.pallas_call(
        place_kernel,
        grid=(4,),
        in_specs=[pl.BlockSpec(memory_space=pltpu.SMEM)] + [full((8, 96, 384))] * 8,
        out_specs=[
            pl.BlockSpec((768, 384), lambda k: (0, k)),
            pl.BlockSpec((768, 384), lambda k: (k // 2, k % 2)),
        ],
        out_shape=[
            jax.ShapeDtypeStruct((768, 1536), F32),
            jax.ShapeDtypeStruct((1536, 768), F32),
        ],
        compiler_params=vmem(32),
        cost_estimate=cost(1 << 20, 14 << 20),
    )(pos, *pieces)


def tail_kernel(
    k0, r0, k1, r1, normed_ref, rstd_ref, frames_ref, segs_ref, stack_ref, cot_ref, kern_ref, gain_ref,
    keep_ref, send_ref, scaled, moved, sums,
):
    sums[...] = jnp.zeros_like(sums)
    taps = [kern_ref[pl.ds(j, 1), :] for j in range(5)]
    gain = gain_ref[...]
    wide_stack = stack_ref[...].astype(F32)
    for j in range(5):
        here = segs_ref[pl.ds(HALO, 128), :]
        same = (segs_ref[pl.ds(HALO - 2 + j, 128), :] == here).astype(F32)
        same = jnp.concatenate([same] * 4, axis=1)
        moved[pl.ds(128 * j, 128), :] = (same * wide_stack[HALO - 2 + j : HALO + 126 + j]).astype(BF)

    def fold(x):
        return x[0:8] + x[8:16]

    for r in range(0, 128, 16):
        at = pl.ds(r, 16)
        dln = jnp.concatenate(
            [k0[at, :].astype(F32) + r0[at, :].astype(F32), k1[at, :].astype(F32) + r1[at, :].astype(F32)], axis=1
        )
        normed = normed_ref[at, :]
        rstd = rstd_ref[at, :][:, 0:1]
        sums[5] += fold(dln * normed)
        dnorm = dln * gain
        m1 = jnp.mean(dnorm, axis=1, keepdims=True)
        m2 = jnp.mean(dnorm * normed, axis=1, keepdims=True)
        dmixed = cot_ref[at, :].astype(F32) + rstd * (dnorm - m1 - normed * m2)
        dmixed = dmixed.astype(BF).astype(F32)
        here = segs_ref[pl.ds(HALO + r, 16), :]
        for j in range(5):
            near = frames_ref[pl.ds(HALO - 2 + r + j, 16), :]
            tap = taps[j]
            if j == 2:
                tap = tap + 1.0
                sums[j] += fold(dmixed * near)
            else:
                same = (segs_ref[pl.ds(HALO - 2 + r + j, 16), :] == here).astype(F32)
                same = jnp.concatenate([same] * 12, axis=1)
                sums[j] += fold(dmixed * (same * near))
            scaled[pl.ds(128 * j + r, 16), :] = (tap * dmixed).astype(BF)

    front = lax.dot_general(
        moved[...], scaled[...], (((0,), (0,)), ((), ())), preferred_element_type=F32
    ).astype(BF)
    for d in range(4):
        keep_ref[pl.ds(64 * d, 64), :] = front[128 * d : 128 * d + 64]
        send_ref[pl.ds(64 * d, 64), :] = front[128 * d + 64 : 128 * d + 128]
    small = jnp.concatenate(
        [jnp.sum(sums[j], axis=0, keepdims=True) for j in range(6)] + [jnp.zeros((2, 1536), F32)], axis=0
    )
    high = small.astype(BF)
    low = (small - high.astype(F32)).astype(BF)
    pair = jnp.concatenate([high.astype(F32), low.astype(F32)], axis=0).astype(BF)
    keep_ref[pl.ds(256, 16), :] = pair
    send_ref[pl.ds(256, 16), :] = pair


def tail(pieces, normed, rstd, frames, segs, stack, cot, kern, gain):
    args = (*pieces, normed, rstd, frames, segs, stack, cot, kern, gain)
    return pl.pallas_call(
        tail_kernel,
        grid=(1,),
        in_specs=[full(a.shape) for a in args],
        out_specs=[full((272, 1536))] * 2,
        out_shape=[jax.ShapeDtypeStruct((272, 1536), BF)] * 2,
        scratch_shapes=[
            pltpu.VMEM((640, 1536), BF), pltpu.VMEM((640, 512), BF), pltpu.VMEM((6, 8, 1536), F32),
        ],
        compiler_params=vmem(32),
        cost_estimate=cost(2 * 640 * 512 * 1536, 6 << 20),
    )(*args)


def split_small(value):
    high = lax.reduce_precision(value, 8, 7)
    return jnp.concatenate([high.astype(BF), (value - high).astype(BF)], axis=0)


def add_rows(pieces, count):
    wide = [p.astype(F32) for p in pieces]
    main = [w[:count] for w in wide]
    small = [w[count : count + 8] + w[count + 8 :] for w in wide]
    if len(wide) == 4:
        pair = lambda v: (v[0] + v[1]) + (v[2] + v[3])
    else:
        pair = lambda v: v[0] + v[1]
    return pair(main), pair(small)


def pack_rows(main, small):
    return jnp.concatenate([main.astype(BF), split_small(small)], axis=0)


def gather_core(value):
    own = jnp.stack([value] + [xor_send(value, "tensor", m, 8) for m in ORDER[1:]])
    return own, xor_send(own, "tensor", 1, 8)


YZ = (("dp", 1), ("context", 1), ("dp", 3), ("context", 3))


def exchange_add(keeps, sends):
    cur, out = list(keeps), list(sends)
    for s in range(4):
        rec = [xor_send(out[k], *YZ[(k + s) % 4], 4) for k in range(4)]
        for k in range(4):
            total = cur[k].astype(F32) + rec[k].astype(F32)
            n = total.shape[0] // 2
            if s < 3:
                cur[k], out[k] = total[:n].astype(BF), total[n:].astype(BF)
            else:
                cur[k] = total.astype(BF)
    pieces = []
    for s in (3, 2, 1, 0):
        rec = [xor_send(cur[k], *YZ[(k + s) % 4], 4) for k in range(4)]
        if s == 0:
            for k in range(4):
                pieces += [cur[k], rec[k]]
        else:
            cur = [jnp.concatenate([cur[k], rec[k]], axis=0) for k in range(4)]
    return pieces


def per_device(
    panels, lengths, segments, front_weight, conv_kernel, gain, up_weight, down_weight, cotangent
):
    y, z, t = lax.axis_index("dp"), lax.axis_index("context"), lax.axis_index("tensor")
    counts = lengths[0]
    before = jnp.arange(4, dtype=jnp.int32) < z
    start = jnp.sum(jnp.where(before, counts, 0))
    count = jnp.sum(jnp.where(jnp.arange(4, dtype=jnp.int32) == z, counts, 0))
    scal = jnp.stack([z, start, count]).astype(jnp.int32)
    order = jnp.stack([t ^ m for m in ORDER] + [t ^ m ^ 1 for m in ORDER]).astype(jnp.int32)
    pos = jnp.stack([y, z]).astype(jnp.int32)
    gain_row = gain[None, :]
    cot = cotangent[0]

    wa, wb = gather_core(front_weight)
    picked = select_panels(scal, jnp.transpose(panels[0, 0], (1, 2, 0)), segments)
    got = [xor_send(picked[e], "context", e, 4) for e in (2, 1, 3)]
    block = picked[0] + got[0] + got[1] + got[2]
    pa, pb = gather_core(block)
    ca, cb = gather_core(cot)
    ca, cb = ca.reshape(512, -1), cb.reshape(512, -1)

    ln, normed, rstd, frames, segs, stack = normalise(order, pa, pb, wa, wb, conv_kernel, gain_row)
    hidden, dpre, dln = feed_forward(ln, ca, cb, up_weight, down_weight)

    dln_rec = xor_send(dln[1], "tensor", 1, 8)
    parts = [weight_part(k, pos, hidden, ca, cb, ln, dpre) for k in range(4)]
    summed = (dln[0].astype(F32) + dln_rec.astype(F32)).astype(BF).reshape(2, 2, 128, 1536)
    send0, send1 = summed[:, 1, :, :768], summed[1, :, :, 768:]
    rec0, rec1 = xor_send(send0, "tensor", 2, 8), xor_send(send1, "tensor", 6, 8)
    sum0 = summed[:, 0, :, :768].astype(F32) + rec0.astype(F32)
    sum1 = summed[0, :, :, 768:].astype(F32) + rec1.astype(F32)
    sum0, sum1 = sum0.astype(BF), sum1.astype(BF)
    end0, end1 = xor_send(sum0[1], "tensor", 6, 8), xor_send(sum1[1], "tensor", 2, 8)

    placed = exchange_add([p[0] for p in parts], [p[1] for p in parts])

    keep, send = tail(
        (sum0[0], end0, sum1[0], end1), normed, rstd, frames, segs, stack, cot, conv_kernel, gain_row
    )
    main, small = add_rows((keep, xor_send(send, "tensor", 1, 8)), 256)
    main = main.astype(BF).reshape(2, 2, 64, 1536)
    pair = split_small(small)

    def payload(blocks, side):
        cols = slice(768 * side, 768 * side + 768)
        return jnp.concatenate([b[..., cols].reshape(-1, 768) for b in blocks] + [pair[:, cols]], axis=0)

    keep0, keep1 = payload([main[:, 0]], 0), payload([main[0]], 1)
    rec0 = xor_send(payload([main[:, 1]], 0), "tensor", 2, 8)
    rec1 = xor_send(payload([main[1]], 1), "tensor", 6, 8)
    ends = []
    for keep_side, rec_side, mask in ((keep0, rec0, 6), (keep1, rec1, 2)):
        value, low = add_rows((keep_side, rec_side), 128)
        low = split_small(low)
        value = value.astype(BF)
        own = jnp.concatenate([value[:64], low], axis=0)
        away = jnp.concatenate([value[64:], low], axis=0)
        ends.append(add_rows((own, xor_send(away, "tensor", mask, 8)), 64))
    value = pack_rows(
        jnp.concatenate([e[0] for e in ends], axis=1), jnp.concatenate([e[1] for e in ends], axis=1)
    )
    for axis in ("context", "dp"):
        near, far, across = [xor_send(value, axis, m, 4) for m in XOR3]
        main, small = add_rows((value, across, near, far), 64)
        if axis == "context":
            value = pack_rows(main, small)
    grad_down, grad_up = place(pos, placed)
    return (main, small[:5], small[5], grad_up, grad_down)


def solution(mesh):
    return jax.shard_map(
        per_device,
        mesh=mesh,
        in_specs=(
            P("dp", "context", None, None, "tensor"),
            P("dp", None),
            P("dp", ("context", "tensor")),
            P("tensor", None),
            P(),
            P(),
            P(None, "tensor"),
            P("tensor", None),
            P("dp", ("context", "tensor"), None),
        ),
        out_specs=(P("tensor", None), P(), P(), P(None, "tensor"), P("tensor", None)),
        check_vma=False,
    )
```

```python
import functools

import jax
import jax.numpy as jnp
from jax import lax
from jax.experimental import pallas as pl
from jax.experimental.pallas import tpu as pltpu
from jax.sharding import PartitionSpec as P

BF = jnp.bfloat16
F32 = jnp.float32
ORDER = (0, 2, 6, 4)
XOR3 = (1, 3, 2)
UNIT = 16
HALO = 16
FIRST = 5 * 10**8


def vmem(limit):
    return pltpu.CompilerParams(vmem_limit_bytes=limit << 20)


def cost(flops, nbytes, trans=0):
    return pl.CostEstimate(flops=flops, bytes_accessed=nbytes, transcendentals=trans)


def full(shape):
    return pl.BlockSpec(shape, lambda *_: (0,) * len(shape))


def fixed(shape):
    return pl.BlockSpec(shape, lambda *_: (0,) * len(shape), pipeline_mode=pl.Buffered(1))


def xor_send(value, axis, mask, size):
    return lax.ppermute(value, axis, [(i, i ^ mask) for i in range(size)])


def select_kernel(lengths, panel_ref, seg_ref, *outs):
    owner = lax.axis_index("context")
    start = jnp.int32(0)
    for shard in range(3):
        start += jnp.where(shard < owner, lengths[0, shard], 0)
    count = lengths[0, owner]
    rows = 40
    slots = panel_ref.shape[2]
    q = lax.broadcasted_iota(jnp.int32, (rows, slots), 0)
    slot = lax.broadcasted_iota(jnp.int32, (rows, slots), 1)
    picks = []
    for e in range(4):
        base = 32 * (owner ^ e)
        wanted = jnp.where(q < 32, base + q, jnp.where(q == 32, base - 1, base + 32))
        inside = (q < 34) & (wanted >= 0) & (wanted < 128)
        local = wanted - start
        hit = inside & (local == slot) & (slot < count)
        picks.append(hit.astype(F32).astype(BF))
    pick = jnp.concatenate(picks, axis=0)
    scratch = outs[4]
    for i in range(UNIT):
        pair = jnp.concatenate([panel_ref[i], panel_ref[i + UNIT]], axis=0)
        got = lax.dot_general(
            pick, pair, (((1,), (1,)), ((), ())), preferred_element_type=F32
        )
        scratch[pl.ds(i, 4 * rows, stride=UNIT), :] = got
    seg_row = seg_ref[...].astype(F32) + 1.0
    for e in range(4):
        target = owner ^ e
        base = e * rows * UNIT
        if e == 0:
            scratch[pl.ds(base + 34 * UNIT, 1), :] = seg_row
        else:
            up = (target == owner + 1).astype(F32)
            down = (target == owner - 1).astype(F32)
            scratch[pl.ds(base + 35 * UNIT, 1), :] = seg_row * up
            scratch[pl.ds(base + 36 * UNIT, 1), :] = seg_row * down
    for e in range(4):
        outs[e][...] = scratch[pl.ds(e * rows * UNIT, rows * UNIT), :].astype(BF)


def select_panels(lengths, panels_t, seg):
    return pl.pallas_call(
        select_kernel,
        out_shape=[jax.ShapeDtypeStruct((640, 128), BF)] * 4,
        in_specs=[
            pl.BlockSpec(memory_space=pltpu.SMEM),
            full(panels_t.shape),
            full(seg.shape),
        ],
        out_specs=[full((640, 128))] * 4,
        grid=(1,),
        scratch_shapes=[pltpu.VMEM((2560, 128), F32)],
        compiler_params=vmem(24),
        cost_estimate=cost(2 * 160 * 65 * 2048, 2 << 20),
    )(lengths, panels_t, seg)


def norm_kernel(
    a_ref, b_ref, wa_ref, wb_ref, kern_ref, gain_ref,
    ln_ref, normed_ref, rstd_ref, frames_ref, segs_ref, stack_ref,
    units, weight, segs, near_segs, wide, near,
):
    step = pl.program_id(0)
    me = lax.axis_index("tensor")

    @pl.when(step == 0)
    def _():
        lane = lax.broadcasted_iota(jnp.int32, (256, 256), 0)
        out_lane = lax.broadcasted_iota(jnp.int32, (256, 256), 1)
        source = (out_lane // 64 % 2) * 128 + (out_lane // 128) * 64 + out_lane % 64
        swap = (lane == source).astype(F32).astype(BF)
        for d in range(4):
            weight[pl.ds(128 * d, 64), :] = wa_ref[d]
            weight[pl.ds(128 * d + 64, 64), :] = wb_ref[d]
            both = jnp.concatenate([a_ref[d, pl.ds(0, 544), :], b_ref[d, pl.ds(0, 544), :]], axis=1)
            mixed = jnp.dot(both, swap, preferred_element_type=F32).astype(BF)
            for p in range(34):
                at = p + 1 if p < 32 else (0 if p == 32 else 33)
                for half in range(2):
                    units[2 * at + half, :, pl.ds(128 * d, 128)] = mixed[
                        16 * p : 16 * p + 16, 128 * half : 128 * half + 128
                    ]
        eye = (
            lax.broadcasted_iota(jnp.int32, (128, 128), 0)
            == lax.broadcasted_iota(jnp.int32, (128, 128), 1)
        ).astype(F32)
        ones = jnp.ones((128, 128), BF)

        def column(ref, d, q):
            row = ref[d, pl.ds(q * UNIT, 16), :].astype(F32)[0:1]
            return jnp.dot((eye * row).astype(BF), ones, preferred_element_type=F32)

        for c in range(2):
            ref = (a_ref, b_ref)[c]
            for d in range(4):
                at = me ^ (ORDER[d] ^ c)
                segs[pl.ds(pl.multiple_of(HALO + 128 * at, 16), 128), :] = column(ref, d, 34)

                @pl.when(at == 7)
                def _():
                    segs[pl.ds(0, HALO), :] = column(ref, d, 35)[128 - HALO :]

                @pl.when(at == 0)
                def _():
                    segs[pl.ds(HALO + 1024, HALO), :] = column(ref, d, 36)[:HALO]

        wide[pl.ds(160, 96), :] = jnp.zeros((96, wide.shape[1]), BF)

    at_step = 7 - step
    spot = lax.rem(at_step, 4)
    block = me ^ (2 * (spot ^ (spot // 2))) ^ (at_step // 4)
    rows = units[pl.ds(8 * block + 1, 10)].reshape(160, 512)
    wide[pl.ds(0, 160), :] = jnp.dot(rows, weight[...], preferred_element_type=F32).astype(BF)
    near_segs[...] = segs[pl.ds(pl.multiple_of(128 * block, 128), 160), :]

    stack_ref[...] = rows
    segs_ref[...] = near_segs[...]

    col = lax.broadcasted_iota(jnp.int32, (128, 256), 1) - lax.broadcasted_iota(jnp.int32, (128, 256), 0)
    here = near_segs[pl.ds(HALO, 128), :]
    shift = []
    for j in (0, 1, 3, 4):
        same = (near_segs[pl.ds(HALO - 2 + j, 128), :] == here).astype(F32)
        same = jnp.concatenate([same, same], axis=1)
        shift.append(jnp.where(col == HALO - 2 + j, same, 0.0).astype(BF))
    near[...] = jnp.dot(jnp.concatenate(shift, axis=0), wide[...], preferred_element_type=F32)

    taps = [kern_ref[pl.ds(j, 1), :] for j in range(5)]
    gain = gain_ref[...]
    for r in range(0, 128, 16):
        mixed = (1.0 + taps[2]) * wide[pl.ds(HALO + r, 16), :].astype(F32)
        for n, j in enumerate((0, 1, 3, 4)):
            mixed = mixed + taps[j] * near[pl.ds(128 * n + r, 16), :]
        mean = jnp.mean(mixed, axis=1, keepdims=True)
        center = mixed - mean
        rstd = lax.rsqrt(jnp.mean(center * center, axis=1, keepdims=True) + 1e-05)
        normed = center * rstd
        ln_ref[pl.ds(r, 16), :] = (normed * gain).astype(BF)
        normed_ref[pl.ds(r, 16), :] = normed
        rstd_ref[pl.ds(r, 16), :] = jnp.broadcast_to(rstd, (16, 128))

    @pl.when(step == 7)
    def _():
        frames_ref[...] = wide[pl.ds(0, 160), :].astype(F32)


def normalise(a, b, wa, wb, kern, gain):
    d_model = kern.shape[1]
    weight = pl.BlockSpec((4, 64, d_model), lambda i: (0, 0, 0))
    return pl.pallas_call(
        norm_kernel,
        grid=(8,),
        in_specs=[full(a.shape), full(b.shape), weight, weight, full(kern.shape), full(gain.shape)],
        out_specs=[
            pl.BlockSpec((128, d_model), lambda i: (7 - i, 0)),
            full((128, d_model)), full((128, 128)), full((160, d_model)),
            full((160, 128)), full((160, 512)),
        ],
        scratch_shapes=[
            pltpu.VMEM((68, 16, 512), BF),
            pltpu.VMEM((512, d_model), BF),
            pltpu.VMEM((1056, 128), F32),
            pltpu.VMEM((160, 128), F32),
            pltpu.VMEM((256, d_model), BF),
            pltpu.VMEM((512, d_model), F32),
        ],
        out_shape=[
            jax.ShapeDtypeStruct((1024, d_model), BF),
            jax.ShapeDtypeStruct((128, d_model), F32),
            jax.ShapeDtypeStruct((128, 128), F32),
            jax.ShapeDtypeStruct((160, d_model), F32),
            jax.ShapeDtypeStruct((160, 128), F32),
            jax.ShapeDtypeStruct((160, 512), BF),
        ],
        compiler_params=vmem(24),
        cost_estimate=cost(12 * 10**9, 10 << 20),
    )(a, b, wa, wb, kern, gain)


def hidden_kernel(ln_ref, up_ref, hid_ref, slope_ref):
    ln = ln_ref[...]
    for c in range(0, up_ref.shape[1], 256):
        part = pl.ds(c, 256)
        pre = jnp.dot(ln, up_ref[:, part], preferred_element_type=F32)
        sig = 1.0 / (1.0 + jnp.exp(-pre))
        hid_ref[:, part] = (pre * sig).astype(BF)
        slope_ref[:, part] = 0.5 * sig * (1.0 + pre * (1.0 - sig))


def hidden_rows(ln, up):
    rows, d_model = ln.shape
    ff = up.shape[1]
    half = rows // 2
    return pl.pallas_call(
        hidden_kernel,
        grid=(2,),
        in_specs=[pl.BlockSpec((half, d_model), lambda i: (i, 0)), fixed(up.shape)],
        out_specs=[pl.BlockSpec((half, ff), lambda i: (i, 0))] * 2,
        out_shape=[jax.ShapeDtypeStruct((rows, ff), BF), jax.ShapeDtypeStruct((rows, ff), F32)],
        compiler_params=vmem(24),
        cost_estimate=cost(2 * rows * d_model * ff, 10 << 20, rows * ff),
    )(ln, up)


def backward_kernel(cot_ref, slope_ref, up_ref, down_ref, dpre_ref, dln_ref):
    cols = (((1,), (1,)), ((), ()))
    grad = cot_ref[...].reshape(dln_ref.shape)
    for c in range(0, up_ref.shape[1], 256):
        part = pl.ds(c, 256)
        dhid = lax.dot_general(grad, down_ref[part, :], cols, preferred_element_type=F32)
        dpre_ref[:, part] = (dhid * slope_ref[:, part]).astype(BF)
    dln_ref[...] = lax.dot_general(
        dpre_ref[...], up_ref[...], cols, preferred_element_type=F32
    ).astype(BF)


def backward_rows(side, cot, slope, up, down):
    d_model, ff = up.shape
    half = slope.shape[0] // 2
    return pl.pallas_call(
        backward_kernel,
        grid=(1,),
        in_specs=[
            full(cot.shape), pl.BlockSpec((half, ff), lambda i: (side, 0)), fixed(up.shape), fixed(down.shape),
        ],
        out_specs=[full((half, ff)), full((half, d_model))],
        out_shape=[jax.ShapeDtypeStruct((half, ff), BF), jax.ShapeDtypeStruct((half, d_model), BF)],
        compiler_params=vmem(32),
        cost_estimate=cost(4 * half * d_model * ff, 10 << 20),
    )(cot, slope, up, down)


PARTS = ((0, 1, 2, 3), (1, 0, 2, 3), (2, 3, 0, 1), (3, 2, 0, 1))
SPREAD = ((0, 1, 2, 3), (1, 2, 3, 0), (2, 3, 0, 1), (3, 0, 1, 2))
YZ = (("dp", 1), ("context", 1), ("dp", 3), ("context", 3))


def piece_code(y, z, r, axes):
    ry, rz = y ^ (r // 4), z ^ (r % 4)
    bits = ((ry & 1) ^ (ry >> 1), (rz & 1) ^ (rz >> 1), ry >> 1, rz >> 1)
    a, b, c, d = (bits[i] for i in axes)
    return (a << 3) | (b << 2) | (c << 1) | d


def weight_kernel(k, hid_ref, ca_ref, cb_ref, ln_ref, da_ref, db_ref, keep_ref, send_ref, both):
    y, z = lax.axis_index("dp"), lax.axis_index("context")
    half = hid_ref.shape[0] // 2
    width = ca_ref.shape[2]
    rows = (((0,), (0,)), ((), ()))
    cot = [ref[...].reshape(half, width) for ref in (ca_ref, cb_ref)]
    down = lax.dot_general(hid_ref[pl.ds(0, half), :], cot[0], rows, preferred_element_type=F32)
    down += lax.dot_general(hid_ref[pl.ds(half, half), :], cot[1], rows, preferred_element_type=F32)
    down = (0.5 * down).astype(BF)
    up = lax.dot_general(ln_ref[pl.ds(0, half), :], da_ref[...], rows, preferred_element_type=F32)
    up += lax.dot_general(ln_ref[pl.ds(half, half), :], db_ref[...], rows, preferred_element_type=F32)
    up = up.astype(BF)
    for r in range(16):
        code = piece_code(y, z, r, PARTS[k])
        both[code, pl.ds(0, 48), :] = down[48 * r : 48 * r + 48]
        both[code, pl.ds(48, 48), :] = up[48 * r : 48 * r + 48]
    keep_ref[...] = both[pl.ds(0, 8)]
    send_ref[...] = both[pl.ds(8, 8)]


def weight_part(k, hidden, ca, cb, ln, dpre_a, dpre_b):
    rows = hidden.shape[0]
    return pl.pallas_call(
        functools.partial(weight_kernel, k),
        grid=(1,),
        in_specs=[
            full((rows, 768)),
            pl.BlockSpec((4, 128, 384), lambda i: (0, 0, k)),
            pl.BlockSpec((4, 128, 384), lambda i: (0, 0, k)),
            pl.BlockSpec((rows, 768), lambda i: (0, k // 2)),
            pl.BlockSpec((rows // 2, 384), lambda i: (0, k % 2)),
            pl.BlockSpec((rows // 2, 384), lambda i: (0, k % 2)),
        ],
        out_specs=[full((8, 96, 384))] * 2,
        out_shape=[jax.ShapeDtypeStruct((8, 96, 384), BF)] * 2,
        scratch_shapes=[pltpu.VMEM((16, 96, 384), BF)],
        compiler_params=vmem(32),
        cost_estimate=cost(4 * rows * 768 * 384, 7 << 20),
    )(hidden, ca, cb, ln, dpre_a, dpre_b)


def place_kernel(*refs):
    ins, (down_ref, up_ref, front_ref, kern_ref, gain_ref) = refs[:8], refs[8:]
    y, z = lax.axis_index("dp"), lax.axis_index("context")
    for k in range(4):

        @pl.when(pl.program_id(0) == k)
        def _():
            pair = ins[2 * k : 2 * k + 2]

            def piece(r, carry):
                code = piece_code(y, z, r, SPREAD[k])
                to = pl.ds(pl.multiple_of(48 * r, 16), 48)
                for side in range(2):

                    @pl.when((code // 8) == side)
                    def _():
                        at = pl.multiple_of((code - 8 * side) * 96, 16)
                        down_ref[to, :] = pair[side][pl.ds(at, 48), :].astype(F32)
                        up_ref[to, :] = pair[side][pl.ds(pl.multiple_of(at + 48, 16), 48), :].astype(F32)

                return carry

            lax.fori_loop(0, 16, piece, 0)
            last = [ref[pl.ds(768, 80), :].astype(F32) for ref in pair]
            front_ref[...] = last[0][:64] + last[1][:64]
            small = (last[0][64:72] + last[0][72:]) + (last[1][64:72] + last[1][72:])
            kern_ref[...] = small[:5]
            gain_ref[...] = small[5:6]


def place(pieces):
    shapes = [(768, 1536), (1536, 768), (64, 1536), (5, 1536), (1, 1536)]
    return pl.pallas_call(
        place_kernel,
        grid=(4,),
        in_specs=[pl.BlockSpec(memory_space=pltpu.VMEM)] * 8,
        out_specs=[
            pl.BlockSpec((768, 384), lambda k: (0, k)),
            pl.BlockSpec((768, 384), lambda k: (k // 2, k % 2)),
            pl.BlockSpec((64, 384), lambda k: (0, k)),
            pl.BlockSpec((5, 384), lambda k: (0, k)),
            pl.BlockSpec((1, 384), lambda k: (0, k)),
        ],
        out_shape=[jax.ShapeDtypeStruct(shape, F32) for shape in shapes],
        compiler_params=vmem(24),
        cost_estimate=cost(1 << 20, 14 << 20),
    )(*pieces)


def high_low(value):
    high = value.astype(BF).astype(F32)
    return jnp.concatenate([high, value - high], axis=0).astype(BF)


def add_small(one, two):
    one, two = one.astype(F32), two.astype(F32)
    return high_low((one[:8] + one[8:]) + (two[:8] + two[8:]))


def tail_kernel(
    k0, r0, k1, r1, normed_ref, rstd_ref, frames_ref, segs_ref, stack_ref, cot_ref, kern_ref, gain_ref,
    keep_ref, send_ref, scaled, moved, sums,
):
    sums[...] = jnp.zeros_like(sums)
    taps = [kern_ref[pl.ds(j, 1), :] for j in range(5)]
    gain = gain_ref[...]
    wide_stack = stack_ref[...].astype(F32)
    for j in range(5):
        here = segs_ref[pl.ds(HALO, 128), :]
        same = (segs_ref[pl.ds(HALO - 2 + j, 128), :] == here).astype(F32)
        same = jnp.concatenate([same] * 4, axis=1)
        moved[pl.ds(128 * j, 128), :] = (same * wide_stack[HALO - 2 + j : HALO + 126 + j]).astype(BF)

    def fold(x):
        return x[0:8] + x[8:16]

    for r in range(0, 128, 16):
        at = pl.ds(r, 16)
        dln = jnp.concatenate(
            [k0[at, :].astype(F32) + r0[at, :].astype(F32), k1[at, :].astype(F32) + r1[at, :].astype(F32)], axis=1
        )
        normed = normed_ref[at, :]
        rstd = rstd_ref[at, :][:, 0:1]
        sums[5] += fold(dln * normed)
        dnorm = dln * gain
        m1 = jnp.mean(dnorm, axis=1, keepdims=True)
        m2 = jnp.mean(dnorm * normed, axis=1, keepdims=True)
        dmixed = cot_ref[at, :].astype(F32) + rstd * (dnorm - m1 - normed * m2)
        dmixed = dmixed.astype(BF).astype(F32)
        here = segs_ref[pl.ds(HALO + r, 16), :]
        for j in range(5):
            near = frames_ref[pl.ds(HALO - 2 + r + j, 16), :]
            tap = taps[j]
            if j == 2:
                tap = tap + 1.0
                sums[j] += fold(dmixed * near)
            else:
                same = (segs_ref[pl.ds(HALO - 2 + r + j, 16), :] == here).astype(F32)
                same = jnp.concatenate([same] * 12, axis=1)
                sums[j] += fold(dmixed * (same * near))
            scaled[pl.ds(128 * j + r, 16), :] = (tap * dmixed).astype(BF)

    front = lax.dot_general(
        moved[...], scaled[...], (((0,), (0,)), ((), ())), preferred_element_type=F32
    )
    for d in range(4):
        keep_ref[pl.ds(64 * d, 64), :] = front[128 * d : 128 * d + 64]
        send_ref[pl.ds(64 * d, 64), :] = front[128 * d + 64 : 128 * d + 128].astype(BF)
    small = jnp.concatenate(
        [jnp.sum(sums[j], axis=0, keepdims=True) for j in range(6)] + [jnp.zeros((2, 1536), F32)], axis=0
    )
    small = high_low(small)
    keep_ref[pl.ds(256, 16), :] = small.astype(F32)
    send_ref[pl.ds(256, 16), :] = small


def tail(pieces, normed, rstd, frames, segs, stack, cot, kern, gain):
    args = (*pieces, normed, rstd, frames, segs, stack, cot, kern, gain)
    return pl.pallas_call(
        tail_kernel,
        grid=(1,),
        in_specs=[full(a.shape) for a in args],
        out_specs=[full((272, 1536))] * 2,
        out_shape=[jax.ShapeDtypeStruct((272, 1536), F32), jax.ShapeDtypeStruct((272, 1536), BF)],
        scratch_shapes=[
            pltpu.VMEM((640, 1536), BF), pltpu.VMEM((640, 512), BF), pltpu.VMEM((6, 8, 1536), F32),
        ],
        compiler_params=vmem(32),
        cost_estimate=cost(60 * 10**9, 6 << 20),
    )(*args)


def gather_core(value):
    own = jnp.stack([value] + [xor_send(value, "tensor", m, 8) for m in ORDER[1:]])
    return own, xor_send(own, "tensor", 1, 8)


def after(value, *others):
    return lax.optimization_barrier((value, *others))[0]


def over(axis, value):
    return xor_send(value, *YZ[axis], 4)


def glue(kernel, outs, *args, flops=5 * 10**8):
    whole = pl.BlockSpec(memory_space=pltpu.VMEM)
    return pl.pallas_call(
        kernel,
        in_specs=[whole] * len(args),
        out_specs=[whole] * len(outs),
        out_shape=[jax.ShapeDtypeStruct(*out) for out in outs],
        compiler_params=vmem(16),
        cost_estimate=cost(flops, 1 << 16),
    )(*args)


def dln_core_kernel(own, rec, keep0, keep1, send0, send1):
    for i in range(4):
        at = pl.ds(128 * i, 128)
        total = own[at, :].astype(F32) + rec[at, :].astype(F32)
        to = pl.ds(128 * (i // 2), 128)
        (send0 if i % 2 else keep0)[to, :] = total[:, :768].astype((send0 if i % 2 else keep0).dtype)
        to = pl.ds(128 * (i % 2), 128)
        (send1 if i // 2 else keep1)[to, :] = total[:, 768:].astype((send1 if i // 2 else keep1).dtype)


def halve_kernel(own, rec, keep, send):
    n = keep.shape[0]
    keep[...] = own[pl.ds(0, n)] + rec[pl.ds(0, n)].astype(F32)
    send[...] = (own[pl.ds(n, n)] + rec[pl.ds(n, n)].astype(F32)).astype(BF)


def halve_first_kernel(own, rec, keep, send):
    n = keep.shape[0]
    keep[...] = own[pl.ds(0, n)].astype(F32) + rec[pl.ds(0, n)].astype(F32)
    send[...] = (own[pl.ds(n, n)].astype(F32) + rec[pl.ds(n, n)].astype(F32)).astype(BF)


def join_kernel(own0, rec0, own1, rec1, keep, send):
    for i, (own, rec) in enumerate(((own0, rec0), (own1, rec1))):
        total = own[...] + rec[...].astype(F32)
        keep[:, pl.ds(96 * i, 96), :] = total[:2]
        send[:, pl.ds(96 * i, 96), :] = total[2:].astype(BF)


def front_core_kernel(own, rec, keep0, keep1, send0, send1):
    for i in range(4):
        at = pl.ds(64 * i, 64)
        total = own[at, :] + rec[at, :].astype(F32)
        to = pl.ds(64 * (i // 2), 64)
        (send0 if i % 2 else keep0)[to, :] = total[:, :768].astype((send0 if i % 2 else keep0).dtype)
        to = pl.ds(64 * (i % 2), 64)
        (send1 if i // 2 else keep1)[to, :] = total[:, 768:].astype((send1 if i // 2 else keep1).dtype)
    small = add_small(own[pl.ds(256, 16), :], rec[pl.ds(256, 16), :])
    for i, (keep, send) in enumerate(((keep0, send0), (keep1, send1))):
        half = small[:, 768 * i : 768 * i + 768]
        keep[pl.ds(128, 16), :] = half.astype(F32)
        send[pl.ds(128, 16), :] = half


def front_x_kernel(own, rec, keep, send):
    keep[pl.ds(0, 64), :] = own[pl.ds(0, 64), :] + rec[pl.ds(0, 64), :].astype(F32)
    send[pl.ds(0, 64), :] = (own[pl.ds(64, 64), :] + rec[pl.ds(64, 64), :].astype(F32)).astype(BF)
    small = add_small(own[pl.ds(128, 16), :], rec[pl.ds(128, 16), :])
    keep[pl.ds(64, 16), :] = small.astype(F32)
    send[pl.ds(64, 16), :] = small


def spread_first_kernel(own, rec, front, front_rec, out0, out1):
    piece = (own[0] + rec[0].astype(F32)).astype(BF)
    front_rows = (front[pl.ds(0, 64), :] + front_rec[pl.ds(0, 64), :].astype(F32)).astype(BF)
    small = add_small(front[pl.ds(64, 16), :], front_rec[pl.ds(64, 16), :])
    for i, out in enumerate((out0, out1)):
        out[pl.ds(0, 96), :] = piece[96 * i : 96 * i + 96]
        out[pl.ds(96, 64), :] = front_rows[:, 384 * i : 384 * i + 384]
        out[pl.ds(160, 16), :] = small[:, 384 * i : 384 * i + 384]


def spread_kernel(own, rec, out):
    n = own.shape[0] - 80
    out[pl.ds(0, n), :] = own[pl.ds(0, n), :]
    out[pl.ds(n, n), :] = rec[pl.ds(0, n), :]
    out[pl.ds(2 * n, 64), :] = (own[pl.ds(n, 64), :].astype(F32) + rec[pl.ds(n, 64), :].astype(F32)).astype(BF)
    out[pl.ds(2 * n + 64, 16), :] = add_small(own[pl.ds(n + 64, 16), :], rec[pl.ds(n + 64, 16), :])


def halve_first(keep, rec):
    return glue(halve_first_kernel, [((4, 96, 384), F32), ((4, 96, 384), BF)], keep, rec)


def reduce_parts(pairs):
    recs = [over(PARTS[k][1], pairs[k][1]) for k in range(4)]
    ends = []
    for k in (0, 2):
        keep, send = glue(
            join_kernel, [((2, 192, 384), F32), ((2, 192, 384), BF)],
            pairs[k][0], recs[k], pairs[k + 1][0], recs[k + 1],
        )
        keep, send = glue(
            halve_kernel, [((1, 192, 384), F32), ((1, 192, 384), BF)], keep, over(PARTS[k][2], send)
        )
        ends.append((keep, over(PARTS[k][3], send)))
    return ends


def spread_parts(ends, fronts):
    bufs = []
    for k in (0, 1):
        bufs += glue(spread_first_kernel, [((176, 384), BF)] * 2, *ends[k], *fronts[k])
    for s in (3, 2, 1):
        recs = [over(SPREAD[k][s], bufs[k]) for k in range(4)]
        rows = 2 * bufs[0].shape[0] - 80
        bufs = [glue(spread_kernel, [((rows, 384), BF)], bufs[k], recs[k])[0] for k in range(4)]
    pieces = []
    for k in range(4):
        pieces += [bufs[k], over(SPREAD[k][0], bufs[k])]
    return pieces


def per_device(
    panels, lengths, segments, front_weight, conv_kernel, gain, up_weight, down_weight, cotangent
):
    gain_row = gain[None, :]
    cot = cotangent[0]

    picked = select_panels(lengths, jnp.transpose(panels[0, 0], (1, 2, 0)), segments)
    *picked, front_weight = lax.optimization_barrier((*picked, front_weight))
    got = [xor_send(picked[e], "context", e, 4) for e in (2, 1, 3)]
    wa, wb = gather_core(front_weight)
    block = picked[0] + got[0] + got[1] + got[2]
    block, cot = lax.optimization_barrier((block, cot))
    pa, pb = gather_core(block)
    others = [xor_send(cot, "tensor", m ^ 1, 8) for m in ORDER]

    ln, normed, rstd, frames, segs, stack = normalise(pa, pb, wa, wb, conv_kernel, gain_row)
    hidden, slope = hidden_rows(ln, up_weight)
    slope, *others = lax.optimization_barrier((slope, *others))
    cb = jnp.stack(others)
    ca = xor_send(cb, "tensor", 1, 8)
    dpre_a, dln_keep = backward_rows(0, ca, slope, up_weight, down_weight)
    dpre_b, dln_send = backward_rows(1, cb, slope, up_weight, down_weight)

    dln_rec = xor_send(dln_send, "tensor", 1, 8)
    k0, k1, s0, s1 = glue(
        dln_core_kernel, [((256, 768), F32)] * 2 + [((256, 768), BF)] * 2, dln_keep, dln_rec
    )
    r0, r1 = xor_send(s0, "tensor", 2, 8), xor_send(s1, "tensor", 6, 8)
    parts = [weight_part(k, hidden, ca, cb, ln, dpre_a, dpre_b) for k in range(4)]
    half = [((128, 768), F32), ((128, 768), BF)]
    k0, s0 = glue(halve_kernel, half, k0, r0)
    k1, s1 = glue(halve_kernel, half, k1, r1)
    pieces = (k0, xor_send(s0, "tensor", 6, 8), k1, xor_send(s1, "tensor", 2, 8))
    keep, send = tail(pieces, normed, rstd, frames, segs, stack, cot, conv_kernel, gain_row)
    pairs = [halve_first(parts[k][0], over(PARTS[k][0], parts[k][1])) for k in range(4)]
    k0, k1, s0, s1 = glue(
        front_core_kernel, [((144, 768), F32)] * 2 + [((144, 768), BF)] * 2,
        keep, xor_send(send, "tensor", 1, 8), flops=FIRST,
    )
    ends = reduce_parts(pairs)
    half = [((80, 768), F32), ((80, 768), BF)]
    k0, s0 = glue(front_x_kernel, half, k0, xor_send(s0, "tensor", 2, 8), flops=FIRST)
    k1, s1 = glue(front_x_kernel, half, k1, xor_send(s1, "tensor", 6, 8), flops=FIRST)
    fronts = (k0, xor_send(s0, "tensor", 6, 8)), (k1, xor_send(s1, "tensor", 2, 8))
    pieces = spread_parts(ends, fronts)
    grad_down, grad_up, grad_front, grad_kernel, grad_gain = place(pieces)
    return (grad_front, grad_kernel, grad_gain[0], grad_up, grad_down)


def solution(mesh):
    return jax.shard_map(
        per_device,
        mesh=mesh,
        in_specs=(
            P("dp", "context", None, None, "tensor"),
            P("dp", None),
            P("dp", ("context", "tensor")),
            P("tensor", None),
            P(),
            P(),
            P(None, "tensor"),
            P("tensor", None),
            P("dp", ("context", "tensor"), None),
        ),
        out_specs=(P("tensor", None), P(), P(), P(None, "tensor"), P("tensor", None)),
        check_vma=False,
    )
```

```python
import functools

import jax
import jax.numpy as jnp
from jax import lax
from jax.experimental import pallas as pl
from jax.experimental.pallas import tpu as pltpu
from jax.sharding import PartitionSpec as P

BF = jnp.bfloat16
F32 = jnp.float32
ORDER = (0, 2, 6, 4)
XOR3 = (1, 3, 2)
UNIT = 16
HALO = 16
FIRST = 5 * 10**8


def vmem(limit):
    return pltpu.CompilerParams(vmem_limit_bytes=limit << 20)


def cost(flops, nbytes, trans=0):
    return pl.CostEstimate(flops=flops, bytes_accessed=nbytes, transcendentals=trans)


def full(shape):
    return pl.BlockSpec(shape, lambda *_: (0,) * len(shape))


WHOLE = pl.BlockSpec(memory_space=pltpu.VMEM)


def xor_send(value, axis, mask, size):
    return lax.ppermute(value, axis, [(i, i ^ mask) for i in range(size)])


def select_kernel(lengths_hbm, panel_hbm, seg_hbm, *outs):
    lengths, panel_ref, seg_ref, sem = outs[5:]
    copies = [
        pltpu.make_async_copy(src, dst, sem.at[i])
        for i, (src, dst) in enumerate(((panel_hbm, panel_ref), (seg_hbm, seg_ref), (lengths_hbm, lengths)))
    ]
    for copy in copies:
        copy.start()
    for copy in copies:
        copy.wait()
    owner = lax.axis_index("context")
    start = jnp.int32(0)
    for shard in range(3):
        start += jnp.where(shard < owner, lengths[0, shard], 0)
    count = lengths[0, owner]
    rows = 40
    slots = panel_ref.shape[2]
    q = lax.broadcasted_iota(jnp.int32, (rows, slots), 0)
    slot = lax.broadcasted_iota(jnp.int32, (rows, slots), 1)
    picks = []
    for e in range(4):
        base = 32 * (owner ^ e)
        wanted = jnp.where(q < 32, base + q, jnp.where(q == 32, base - 1, base + 32))
        inside = (q < 34) & (wanted >= 0) & (wanted < 128)
        local = wanted - start
        hit = inside & (local == slot) & (slot < count)
        picks.append(hit.astype(F32).astype(BF))
    pick = jnp.concatenate(picks, axis=0)
    scratch = outs[4]
    for i in range(UNIT):
        pair = jnp.concatenate([panel_ref[i], panel_ref[i + UNIT]], axis=0)
        got = lax.dot_general(
            pick, pair, (((1,), (1,)), ((), ())), preferred_element_type=F32
        )
        scratch[pl.ds(i, 4 * rows, stride=UNIT), :] = got
    seg_row = seg_ref[...].astype(F32) + 1.0
    for e in range(4):
        target = owner ^ e
        base = e * rows * UNIT
        if e == 0:
            scratch[pl.ds(base + 34 * UNIT, 1), :] = seg_row
        else:
            up = (target == owner + 1).astype(F32)
            down = (target == owner - 1).astype(F32)
            scratch[pl.ds(base + 35 * UNIT, 1), :] = seg_row * up
            scratch[pl.ds(base + 36 * UNIT, 1), :] = seg_row * down
    for e in range(4):
        outs[e][...] = scratch[pl.ds(e * rows * UNIT, rows * UNIT), :].astype(BF)


def select_panels(lengths, panels_t, seg):
    return pl.pallas_call(
        select_kernel,
        out_shape=[jax.ShapeDtypeStruct((640, 128), BF)] * 4,
        in_specs=[pl.BlockSpec(memory_space=pl.ANY)] * 3,
        out_specs=[WHOLE] * 4,
        scratch_shapes=[
            pltpu.VMEM((2560, 128), F32),
            pltpu.SMEM(lengths.shape, jnp.int32),
            pltpu.VMEM(panels_t.shape, BF),
            pltpu.VMEM(seg.shape, jnp.int32),
            pltpu.SemaphoreType.DMA((3,)),
        ],
        compiler_params=vmem(56),
        cost_estimate=cost(2 * 160 * 65 * 2048, 2 << 20),
    )(lengths, panels_t, seg)


def norm_kernel(
    a_ref, b_ref, wa_ref, wb_ref, kern_ref, gain_ref,
    ln_ref, normed_ref, rstd_ref, frames_ref, segs_ref, stack_ref,
    units, weight, segs, *blocks,
):
    step = pl.program_id(0)
    me = lax.axis_index("tensor")

    @pl.when(step == 0)
    def _():
        lane = lax.broadcasted_iota(jnp.int32, (256, 256), 0)
        out_lane = lax.broadcasted_iota(jnp.int32, (256, 256), 1)
        source = (out_lane // 64 % 2) * 128 + (out_lane // 128) * 64 + out_lane % 64
        swap = (lane == source).astype(F32).astype(BF)
        for d in range(4):
            weight[pl.ds(128 * d, 64), :] = wa_ref[d]
            weight[pl.ds(128 * d + 64, 64), :] = wb_ref[d]
            both = jnp.concatenate([a_ref[d, pl.ds(0, 544), :], b_ref[d, pl.ds(0, 544), :]], axis=1)
            mixed = jnp.dot(both, swap, preferred_element_type=F32).astype(BF)
            for p in range(34):
                at = p + 1 if p < 32 else (0 if p == 32 else 33)
                for half in range(2):
                    units[2 * at + half, :, pl.ds(128 * d, 128)] = mixed[
                        16 * p : 16 * p + 16, 128 * half : 128 * half + 128
                    ]
        eye = (
            lax.broadcasted_iota(jnp.int32, (128, 128), 0)
            == lax.broadcasted_iota(jnp.int32, (128, 128), 1)
        ).astype(F32)
        ones = jnp.ones((128, 128), BF)

        def column(ref, d, q):
            row = ref[d, pl.ds(q * UNIT, 16), :].astype(F32)[0:1]
            return jnp.dot((eye * row).astype(BF), ones, preferred_element_type=F32)

        for c in range(2):
            ref = (a_ref, b_ref)[c]
            for d in range(4):
                at = me ^ (ORDER[d] ^ c)
                segs[pl.ds(pl.multiple_of(HALO + 128 * at, 16), 128), :] = column(ref, d, 34)

                @pl.when(at == 7)
                def _():
                    segs[pl.ds(0, HALO), :] = column(ref, d, 35)[128 - HALO :]

                @pl.when(at == 0)
                def _():
                    segs[pl.ds(HALO + 1024, HALO), :] = column(ref, d, 36)[:HALO]

        for wide in (blocks[1], blocks[4]):
            wide[pl.ds(160, 96), :] = jnp.zeros((96, wide.shape[1]), BF)

    outs = (ln_ref, normed_ref, rstd_ref, segs_ref, stack_ref)
    for i in range(2):
        norm_block(me, 7 - 2 * step - i, kern_ref, gain_ref, units, weight, segs, *blocks[3 * i : 3 * i + 3], *outs)

    @pl.when(step == 3)
    def _():
        frames_ref[...] = blocks[4][pl.ds(0, 160), :].astype(F32)


def norm_block(
    me, at_step, kern_ref, gain_ref, units, weight, segs, near_segs, wide, near,
    ln_ref, normed_ref, rstd_ref, segs_ref, stack_ref,
):
    spot = lax.rem(at_step, 4)
    block = me ^ (2 * (spot ^ (spot // 2))) ^ (at_step // 4)
    rows = units[pl.ds(8 * block + 1, 10)].reshape(160, 512)
    wide[pl.ds(0, 160), :] = jnp.dot(rows, weight[...], preferred_element_type=F32).astype(BF)
    near_segs[...] = segs[pl.ds(pl.multiple_of(128 * block, 128), 160), :]

    stack_ref[...] = rows
    segs_ref[...] = near_segs[...]

    col = lax.broadcasted_iota(jnp.int32, (128, 256), 1) - lax.broadcasted_iota(jnp.int32, (128, 256), 0)
    here = near_segs[pl.ds(HALO, 128), :]
    shift = []
    for j in (0, 1, 3, 4):
        same = (near_segs[pl.ds(HALO - 2 + j, 128), :] == here).astype(F32)
        same = jnp.concatenate([same, same], axis=1)
        shift.append(jnp.where(col == HALO - 2 + j, same, 0.0).astype(BF))
    near[...] = jnp.dot(jnp.concatenate(shift, axis=0), wide[...], preferred_element_type=F32)

    taps = [kern_ref[pl.ds(j, 1), :] for j in range(5)]
    gain = gain_ref[...]
    for r in range(0, 128, 16):
        mixed = (1.0 + taps[2]) * wide[pl.ds(HALO + r, 16), :].astype(F32)
        for n, j in enumerate((0, 1, 3, 4)):
            mixed = mixed + taps[j] * near[pl.ds(128 * n + r, 16), :]
        mean = jnp.mean(mixed, axis=1, keepdims=True)
        center = mixed - mean
        rstd = lax.rsqrt(jnp.mean(center * center, axis=1, keepdims=True) + 1e-05)
        normed = center * rstd
        ln_ref[pl.ds(pl.multiple_of(128 * at_step + r, 16), 16), :] = (normed * gain).astype(BF)
        normed_ref[pl.ds(r, 16), :] = normed
        rstd_ref[pl.ds(r, 16), :] = jnp.broadcast_to(rstd, (16, 128))


def normalise(a, b, wa, wb, kern, gain):
    d_model = kern.shape[1]
    return pl.pallas_call(
        norm_kernel,
        grid=(4,),
        in_specs=[WHOLE] * 6,
        out_specs=[WHOLE] * 6,
        scratch_shapes=[
            pltpu.VMEM((68, 16, 512), BF),
            pltpu.VMEM((512, d_model), BF),
            pltpu.VMEM((1056, 128), F32),
        ]
        + [
            pltpu.VMEM((160, 128), F32),
            pltpu.VMEM((256, d_model), BF),
            pltpu.VMEM((512, d_model), F32),
        ]
        * 2,
        out_shape=[
            jax.ShapeDtypeStruct((1024, d_model), BF),
            jax.ShapeDtypeStruct((128, d_model), F32),
            jax.ShapeDtypeStruct((128, 128), F32),
            jax.ShapeDtypeStruct((160, d_model), F32),
            jax.ShapeDtypeStruct((160, 128), F32),
            jax.ShapeDtypeStruct((160, 512), BF),
        ],
        compiler_params=vmem(20),
        cost_estimate=cost(12 * 10**9, 10 << 20),
    )(a, b, wa, wb, kern, gain)


def hidden_kernel(ln_ref, up_ref, down_ref, hid_ref, slope_ref):
    del down_ref
    half = ln_ref.shape[0] // 2

    def block(r, carry):
        rows = pl.ds(pl.multiple_of(half * r, 128), half)
        for c in range(0, up_ref.shape[1], 256):
            part = pl.ds(c, 256)
            pre = jnp.dot(ln_ref[rows, :], up_ref[:, part], preferred_element_type=F32)
            sig = 1.0 / (1.0 + jnp.exp(-pre))
            hid_ref[rows, part] = (pre * sig).astype(BF)
            slope_ref[rows, part] = 0.5 * sig * (1.0 + pre * (1.0 - sig))
        return carry

    lax.fori_loop(0, 2, block, 0)


def hidden_rows(ln, up, down):
    rows, d_model = ln.shape
    ff = up.shape[1]
    return pl.pallas_call(
        hidden_kernel,
        in_specs=[WHOLE] * 3,
        out_specs=[WHOLE] * 2,
        out_shape=[jax.ShapeDtypeStruct((rows, ff), BF), jax.ShapeDtypeStruct((rows, ff), F32)],
        compiler_params=vmem(12),
        cost_estimate=cost(2 * rows * d_model * ff, 10 << 20, rows * ff),
    )(ln, up, down)


def backward_kernel(side, cot_ref, slope_ref, up_ref, down_ref, dpre_ref, dln_ref):
    cols = (((1,), (1,)), ((), ()))
    rows = dln_ref.shape[0]
    grad = cot_ref[...].reshape(dln_ref.shape)
    for c in range(0, up_ref.shape[1], 256):
        part = pl.ds(c, 256)
        dhid = lax.dot_general(grad, down_ref[part, :], cols, preferred_element_type=F32)
        dpre_ref[:, part] = (dhid * slope_ref[pl.ds(rows * side, rows), part]).astype(BF)
    dln_ref[...] = lax.dot_general(
        dpre_ref[...], up_ref[...], cols, preferred_element_type=F32
    ).astype(BF)


def backward_rows(side, cot, slope, up, down):
    d_model, ff = up.shape
    half = slope.shape[0] // 2
    return pl.pallas_call(
        functools.partial(backward_kernel, side),
        in_specs=[WHOLE] * 4,
        out_specs=[WHOLE] * 2,
        out_shape=[jax.ShapeDtypeStruct((half, ff), BF), jax.ShapeDtypeStruct((half, d_model), BF)],
        compiler_params=vmem(12),
        cost_estimate=cost(4 * half * d_model * ff, 10 << 20),
    )(cot, slope, up, down)


PARTS = ((0, 1, 2, 3), (1, 0, 2, 3), (2, 3, 0, 1), (3, 2, 0, 1))
SPREAD = ((0, 1, 2, 3), (1, 2, 3, 0), (2, 3, 0, 1), (3, 0, 1, 2))
YZ = (("dp", 1), ("context", 1), ("dp", 3), ("context", 3))


def piece_code(y, z, r, axes):
    ry, rz = y ^ (r // 4), z ^ (r % 4)
    bits = ((ry & 1) ^ (ry >> 1), (rz & 1) ^ (rz >> 1), ry >> 1, rz >> 1)
    a, b, c, d = (bits[i] for i in axes)
    return (a << 3) | (b << 2) | (c << 1) | d


def weight_kernel(k, hid_ref, ca_ref, cb_ref, ln_ref, da_ref, db_ref, keep_ref, send_ref, both):
    y, z = lax.axis_index("dp"), lax.axis_index("context")
    half = hid_ref.shape[0] // 2
    cols, wide_cols, ff_cols = pl.ds(384 * k, 384), pl.ds(768 * (k // 2), 768), pl.ds(384 * (k % 2), 384)
    rows = (((0,), (0,)), ((), ()))
    cot = [ref[:, :, cols].reshape(half, 384) for ref in (ca_ref, cb_ref)]
    down = lax.dot_general(hid_ref[pl.ds(0, half), :], cot[0], rows, preferred_element_type=F32)
    down += lax.dot_general(hid_ref[pl.ds(half, half), :], cot[1], rows, preferred_element_type=F32)
    down = (0.5 * down).astype(BF)
    up = lax.dot_general(ln_ref[pl.ds(0, half), wide_cols], da_ref[:, ff_cols], rows, preferred_element_type=F32)
    up += lax.dot_general(ln_ref[pl.ds(half, half), wide_cols], db_ref[:, ff_cols], rows, preferred_element_type=F32)
    up = up.astype(BF)
    for r in range(16):
        code = piece_code(y, z, r, PARTS[k])
        both[code, pl.ds(0, 48), :] = down[48 * r : 48 * r + 48]
        both[code, pl.ds(48, 48), :] = up[48 * r : 48 * r + 48]
    keep_ref[...] = both[pl.ds(0, 8)]
    send_ref[...] = both[pl.ds(8, 8)]


def weight_part(k, hidden, ca, cb, ln, dpre_a, dpre_b):
    rows = hidden.shape[0]
    return pl.pallas_call(
        functools.partial(weight_kernel, k),
        in_specs=[WHOLE] * 6,
        out_specs=[WHOLE] * 2,
        out_shape=[jax.ShapeDtypeStruct((8, 96, 384), BF)] * 2,
        scratch_shapes=[pltpu.VMEM((16, 96, 384), BF)],
        compiler_params=vmem(14),
        cost_estimate=cost(4 * rows * 768 * 384, 7 << 20),
    )(hidden, ca, cb, ln, dpre_a, dpre_b)


def piece_row(y, z, code, axes):
    bits = [0] * 4
    for i, axis in enumerate(axes):
        bits[axis] = (code >> (3 - i)) & 1
    ay, az, by, bz = bits
    return 4 * (y ^ (2 * by | (ay ^ by))) + (z ^ (2 * bz | (az ^ bz)))


def place_pieces(side, bufs, down_ref, up_ref, stage, sems):
    y, z = lax.axis_index("dp"), lax.axis_index("context")
    copies = []
    for k in range(4):
        for c in range(8):
            row = 48 * piece_row(y, z, 8 * side + c, SPREAD[k])
            for i, (out, row0, col0) in enumerate(((down_ref, 0, 384 * k), (up_ref, 768 * (k // 2), 384 * (k % 2)))):
                stage[k, c, i] = bufs[k][pl.ds(96 * c + 48 * i, 48), :].astype(F32)
                to = out.at[pl.ds(pl.multiple_of(row0 + row, 16), 48), pl.ds(col0, 384)]
                copies.append(pltpu.make_async_copy(stage.at[k, c, i], to, sems.at[k, c, i]))
                copies[-1].start()
    return copies


def place_own_kernel(*refs):
    for copy in place_pieces(0, refs[:4], *refs[4:]):
        copy.wait()


def place_rest_kernel(*refs):
    own, rec = refs[:4], refs[4:8]
    down_ref, up_ref, front_ref, kern_ref, gain_ref, stage, sems = refs[10:]
    copies = place_pieces(1, rec, down_ref, up_ref, stage, sems)
    for k in range(4):
        last = [ref[pl.ds(768, 80), :].astype(F32) for ref in (own[k], rec[k])]
        cols = pl.ds(384 * k, 384)
        front_ref[:, cols] = last[0][:64] + last[1][:64]
        small = (last[0][64:72] + last[0][72:]) + (last[1][64:72] + last[1][72:])
        kern_ref[:, cols] = small[:5]
        gain_ref[cols] = small[5]
    for copy in copies:
        copy.wait()


def place(own, rec):
    big = [jax.ShapeDtypeStruct((768, 1536), F32), jax.ShapeDtypeStruct((1536, 768), F32)]
    hbm = pl.BlockSpec(memory_space=pl.ANY)
    small = [(64, 1536), (5, 1536), (1536,)]
    scratch = [pltpu.VMEM((4, 8, 2, 48, 384), F32), pltpu.SemaphoreType.DMA((4, 8, 2))]
    started = pl.pallas_call(
        place_own_kernel,
        in_specs=[WHOLE] * 4,
        out_specs=[hbm] * 2,
        out_shape=big,
        scratch_shapes=scratch,
        compiler_params=vmem(40),
        cost_estimate=cost(1 << 20, 7 << 20),
    )(*own)
    return pl.pallas_call(
        place_rest_kernel,
        grid=(1,),
        in_specs=[WHOLE] * 8 + [hbm] * 2,
        out_specs=[hbm] * 2 + [full(shape) for shape in small],
        out_shape=big + [jax.ShapeDtypeStruct(shape, F32) for shape in small],
        input_output_aliases={8: 0, 9: 1},
        scratch_shapes=scratch,
        compiler_params=vmem(40),
        cost_estimate=cost(1 << 20, 7 << 20),
    )(*own, *rec, *started)


def high_low(value):
    high = value.astype(BF).astype(F32)
    return jnp.concatenate([high, value - high], axis=0).astype(BF)


def add_small(one, two):
    one, two = one.astype(F32), two.astype(F32)
    return high_low((one[:8] + one[8:]) + (two[:8] + two[8:]))


def tail_kernel(
    dln_ref, rec_ref, normed_ref, rstd_ref, frames_ref, segs_ref, stack_ref, cot_ref, kern_ref, gain_ref,
    keep_ref, send_ref, scaled, moved, sums,
):
    sums[...] = jnp.zeros_like(sums)
    taps = [kern_ref[pl.ds(j, 1), :] for j in range(5)]
    gain = gain_ref[...]
    wide_stack = stack_ref[...].astype(F32)
    for j in range(5):
        here = segs_ref[pl.ds(HALO, 128), :]
        same = (segs_ref[pl.ds(HALO - 2 + j, 128), :] == here).astype(F32)
        same = jnp.concatenate([same] * 4, axis=1)
        moved[pl.ds(128 * j, 128), :] = (same * wide_stack[HALO - 2 + j : HALO + 126 + j]).astype(BF)

    def fold(x):
        return x[0:8] + x[8:16]

    for r in range(0, 128, 16):
        at = pl.ds(r, 16)
        dln = dln_ref[at, :] + rec_ref[at, :].astype(F32)
        normed = normed_ref[at, :]
        rstd = rstd_ref[at, :][:, 0:1]
        sums[5] += fold(dln * normed)
        dnorm = dln * gain
        m1 = jnp.mean(dnorm, axis=1, keepdims=True)
        m2 = jnp.mean(dnorm * normed, axis=1, keepdims=True)
        dmixed = cot_ref[at, :].astype(F32) + rstd * (dnorm - m1 - normed * m2)
        dmixed = dmixed.astype(BF).astype(F32)
        here = segs_ref[pl.ds(HALO + r, 16), :]
        for j in range(5):
            near = frames_ref[pl.ds(HALO - 2 + r + j, 16), :]
            tap = taps[j]
            if j == 2:
                tap = tap + 1.0
                sums[j] += fold(dmixed * near)
            else:
                same = (segs_ref[pl.ds(HALO - 2 + r + j, 16), :] == here).astype(F32)
                same = jnp.concatenate([same] * 12, axis=1)
                sums[j] += fold(dmixed * (same * near))
            scaled[pl.ds(128 * j + r, 16), :] = (tap * dmixed).astype(BF)

    front = lax.dot_general(
        moved[...], scaled[...], (((0,), (0,)), ((), ())), preferred_element_type=F32
    )
    for d in range(4):
        keep_ref[pl.ds(64 * d, 64), :] = front[128 * d : 128 * d + 64]
        send_ref[pl.ds(64 * d, 64), :] = front[128 * d + 64 : 128 * d + 128].astype(BF)
    small = jnp.concatenate(
        [jnp.sum(sums[j], axis=0, keepdims=True) for j in range(6)] + [jnp.zeros((2, 1536), F32)], axis=0
    )
    small = high_low(small)
    keep_ref[pl.ds(256, 16), :] = small.astype(F32)
    send_ref[pl.ds(256, 16), :] = small


def tail(pieces, normed, rstd, frames, segs, stack, cot, kern, gain):
    args = (*pieces, normed, rstd, frames, segs, stack, cot, kern, gain)
    return pl.pallas_call(
        tail_kernel,
        in_specs=[WHOLE] * len(args),
        out_specs=[WHOLE] * 2,
        out_shape=[jax.ShapeDtypeStruct((272, 1536), F32), jax.ShapeDtypeStruct((272, 1536), BF)],
        scratch_shapes=[
            pltpu.VMEM((640, 1536), BF), pltpu.VMEM((640, 512), BF), pltpu.VMEM((6, 8, 1536), F32),
        ],
        compiler_params=vmem(16),
        cost_estimate=cost(60 * 10**9, 6 << 20),
    )(*args)


def gather_core(value):
    own = jnp.stack([value] + [xor_send(value, "tensor", m, 8) for m in ORDER[1:]])
    return own, xor_send(own, "tensor", 1, 8)


def after(value, *others):
    return lax.optimization_barrier((value, *others))[0]


def over(axis, value):
    return xor_send(value, *YZ[axis], 4)


def glue(kernel, outs, *args, flops=5 * 10**8):
    return pl.pallas_call(
        kernel,
        in_specs=[WHOLE] * len(args),
        out_specs=[WHOLE] * len(outs),
        out_shape=[jax.ShapeDtypeStruct(*out) for out in outs],
        compiler_params=vmem(16),
        cost_estimate=cost(flops, 1 << 16),
    )(*args)


def dln_core_kernel(own, rec, keep, send):
    for i in range(4):
        at, to = pl.ds(128 * i, 128), pl.ds(128 * (i // 2), 128)
        total = own[at, :].astype(F32) + rec[at, :].astype(F32)
        if i % 2:
            send[to, :] = total.astype(BF)
        else:
            keep[to, :] = total


def halve_kernel(own, rec, keep, send):
    n = keep.shape[0]
    keep[...] = own[pl.ds(0, n)] + rec[pl.ds(0, n)].astype(F32)
    send[...] = (own[pl.ds(n, n)] + rec[pl.ds(n, n)].astype(F32)).astype(BF)


def halve_first_kernel(own, rec, keep, send):
    n = keep.shape[0]
    keep[...] = own[pl.ds(0, n)].astype(F32) + rec[pl.ds(0, n)].astype(F32)
    send[...] = (own[pl.ds(n, n)].astype(F32) + rec[pl.ds(n, n)].astype(F32)).astype(BF)


def join_kernel(own0, rec0, own1, rec1, keep, send):
    for i, (own, rec) in enumerate(((own0, rec0), (own1, rec1))):
        total = own[...] + rec[...].astype(F32)
        keep[:, pl.ds(96 * i, 96), :] = total[:2]
        send[:, pl.ds(96 * i, 96), :] = total[2:].astype(BF)


def front_core_kernel(own, rec, keep0, keep1, send0, send1):
    for i in range(4):
        at = pl.ds(64 * i, 64)
        total = own[at, :] + rec[at, :].astype(F32)
        out = send0 if i % 2 else keep0
        out[pl.ds(64 * (i // 2), 64), :] = total[:, :768].astype(out.dtype)
        out = send1 if i // 2 else keep1
        out[pl.ds(64 * (i % 2), 64), :] = total[:, 768:].astype(out.dtype)
    small = add_small(own[pl.ds(256, 16), :], rec[pl.ds(256, 16), :])
    for i, (keep, send) in enumerate(((keep0, send0), (keep1, send1))):
        half = small[:, 768 * i : 768 * i + 768]
        keep[pl.ds(128, 16), :] = half.astype(F32)
        send[pl.ds(128, 16), :] = half


def front_x_kernel(own, rec, keep, send):
    keep[pl.ds(0, 64), :] = own[pl.ds(0, 64), :] + rec[pl.ds(0, 64), :].astype(F32)
    send[pl.ds(0, 64), :] = (own[pl.ds(64, 64), :] + rec[pl.ds(64, 64), :].astype(F32)).astype(BF)
    small = add_small(own[pl.ds(128, 16), :], rec[pl.ds(128, 16), :])
    keep[pl.ds(64, 16), :] = small.astype(F32)
    send[pl.ds(64, 16), :] = small


def spread_first_kernel(own, rec, front, front_rec, out0, out1):
    piece = (own[0] + rec[0].astype(F32)).astype(BF)
    front_rows = (front[pl.ds(0, 64), :] + front_rec[pl.ds(0, 64), :].astype(F32)).astype(BF)
    small = add_small(front[pl.ds(64, 16), :], front_rec[pl.ds(64, 16), :])
    for i, out in enumerate((out0, out1)):
        out[pl.ds(0, 96), :] = piece[96 * i : 96 * i + 96]
        cols = slice(384 * i, 384 * i + 384)
        out[pl.ds(96, 64), :] = front_rows[:, cols]
        out[pl.ds(160, 16), :] = small[:, cols]


def spread_kernel(own, rec, out):
    n = own.shape[0] - 80
    out[pl.ds(0, n), :] = own[pl.ds(0, n), :]
    out[pl.ds(n, n), :] = rec[pl.ds(0, n), :]
    out[pl.ds(2 * n, 64), :] = (own[pl.ds(n, 64), :].astype(F32) + rec[pl.ds(n, 64), :].astype(F32)).astype(BF)
    out[pl.ds(2 * n + 64, 16), :] = add_small(own[pl.ds(n + 64, 16), :], rec[pl.ds(n + 64, 16), :])


def halve_first(keep, rec):
    return glue(halve_first_kernel, [((4, 96, 384), F32), ((4, 96, 384), BF)], keep, rec)


def join_parts(k, pairs, recs):
    return glue(
        join_kernel, [((2, 192, 384), F32), ((2, 192, 384), BF)],
        pairs[k][0], recs[0], pairs[k + 1][0], recs[1],
    )


def reduce_ends(k, keep, send):
    keep, send = glue(
        halve_kernel, [((1, 192, 384), F32), ((1, 192, 384), BF)], keep, over(PARTS[k][2], send)
    )
    return keep, over(PARTS[k][3], send)


def spread_parts(ends, fronts):
    bufs = []
    for k in (0, 1):
        bufs += glue(spread_first_kernel, [((176, 384), BF)] * 2, *ends[k], *fronts[k])
    for s in (3, 2, 1):
        recs = [over(SPREAD[k][s], bufs[k]) for k in range(4)]
        rows = 2 * bufs[0].shape[0] - 80
        bufs = [glue(spread_kernel, [((rows, 384), BF)], bufs[k], recs[k])[0] for k in range(4)]
    return bufs, [over(SPREAD[k][0], bufs[k]) for k in range(4)]


def per_device(
    panels, lengths, segments, front_weight, conv_kernel, gain, up_weight, down_weight, cotangent
):
    gain_row = gain[None, :]
    cot = cotangent[0]

    picked = select_panels(lengths, jnp.transpose(panels[0, 0], (1, 2, 0)), segments)
    *picked, front_weight = lax.optimization_barrier((*picked, front_weight))
    got = [xor_send(picked[e], "context", e, 4) for e in (2, 1, 3)]
    wa, wb = gather_core(front_weight)
    block = picked[0] + got[0] + got[1] + got[2]
    block, cot = lax.optimization_barrier((block, cot))
    pa, pb = gather_core(block)
    others = [xor_send(cot, "tensor", m ^ 1, 8) for m in ORDER]

    ln, normed, rstd, frames, segs, stack = normalise(pa, pb, wa, wb, conv_kernel, gain_row)
    hidden, slope = hidden_rows(ln, up_weight, down_weight)
    slope, *others = lax.optimization_barrier((slope, *others))
    cb = jnp.stack(others)
    ca = xor_send(cb, "tensor", 1, 8)
    dpre_a, dln_keep = backward_rows(0, ca, slope, up_weight, down_weight)
    dpre_b, dln_send = backward_rows(1, cb, slope, up_weight, down_weight)

    dln_rec = xor_send(dln_send, "tensor", 1, 8)
    keep, send = glue(
        dln_core_kernel, [((256, 1536), F32), ((256, 1536), BF)], dln_keep, dln_rec
    )
    rec = xor_send(send, "tensor", 2, 8)
    parts = [weight_part(k, hidden, ca, cb, ln, dpre_a, dpre_b) for k in range(4)]
    firsts = [over(PARTS[k][0], parts[k][1]) for k in range(4)]
    pairs = [halve_first(parts[0][0], firsts[0])]
    rec = after(rec, pairs[0][1], *[p[0] for p in parts[1:]])
    keep, send = glue(halve_kernel, [((128, 1536), F32), ((128, 1536), BF)], keep, rec)
    pairs.append(halve_first(parts[1][0], firsts[1]))
    send = after(send, pairs[1][1])
    rec = xor_send(send, "tensor", 6, 8)
    pairs += [halve_first(parts[k][0], firsts[k]) for k in (2, 3)]
    seconds = [over(PARTS[k][1], pairs[k][1]) for k in range(4)]
    joined = join_parts(0, pairs, seconds[:2])
    pieces = (keep, after(rec, joined[1], *seconds[2:]))
    keep, send = tail(pieces, normed, rstd, frames, segs, stack, cot, conv_kernel, gain_row)
    ends = reduce_ends(0, *joined), reduce_ends(2, *join_parts(2, pairs, seconds[2:]))
    k0, k1, s0, s1 = glue(
        front_core_kernel, [((144, 768), F32)] * 2 + [((144, 768), BF)] * 2,
        keep, xor_send(send, "tensor", 1, 8), flops=FIRST,
    )
    half = [((80, 768), F32), ((80, 768), BF)]
    k0, s0 = glue(front_x_kernel, half, k0, xor_send(s0, "tensor", 2, 8), flops=FIRST)
    k1, s1 = glue(front_x_kernel, half, k1, xor_send(s1, "tensor", 6, 8), flops=FIRST)
    fronts = (k0, xor_send(s0, "tensor", 6, 8)), (k1, xor_send(s1, "tensor", 2, 8))
    own, rec = spread_parts(ends, fronts)
    grad_down, grad_up, grad_front, grad_kernel, grad_gain = place(own, rec)
    return (grad_front, grad_kernel, grad_gain, grad_up, grad_down)


def solution(mesh):
    return jax.shard_map(
        per_device,
        mesh=mesh,
        in_specs=(
            P("dp", "context", None, None, "tensor"),
            P("dp", None),
            P("dp", ("context", "tensor")),
            P("tensor", None),
            P(),
            P(),
            P(None, "tensor"),
            P("tensor", None),
            P("dp", ("context", "tensor"), None),
        ),
        out_specs=(P("tensor", None), P(), P(), P(None, "tensor"), P("tensor", None)),
        check_vma=False,
    )
```

```python
import functools

import jax
import jax.numpy as jnp
from jax import lax
from jax.experimental import pallas as pl
from jax.experimental.pallas import tpu as pltpu
from jax.sharding import PartitionSpec as P

BF = jnp.bfloat16
F32 = jnp.float32
ORDER = (0, 2, 6, 4)
XOR3 = (1, 3, 2)
UNIT = 16
HALO = 16
FIRST = 5 * 10**8


def vmem(limit):
    return pltpu.CompilerParams(vmem_limit_bytes=limit << 20)


def cost(flops, nbytes, trans=0):
    return pl.CostEstimate(flops=flops, bytes_accessed=nbytes, transcendentals=trans)


def full(shape):
    return pl.BlockSpec(shape, lambda *_: (0,) * len(shape))


WHOLE = pl.BlockSpec(memory_space=pltpu.VMEM)


def xor_send(value, axis, mask, size):
    return lax.ppermute(value, axis, [(i, i ^ mask) for i in range(size)])


def select_kernel(lengths_hbm, panel_hbm, seg_hbm, *outs):
    lengths, panel_ref, seg_ref, sem = outs[5:]
    copies = [
        pltpu.make_async_copy(src, dst, sem.at[i])
        for i, (src, dst) in enumerate(((panel_hbm, panel_ref), (seg_hbm, seg_ref), (lengths_hbm, lengths)))
    ]
    for copy in copies:
        copy.start()
    for copy in copies:
        copy.wait()
    owner = lax.axis_index("context")
    start = jnp.int32(0)
    for shard in range(3):
        start += jnp.where(shard < owner, lengths[0, shard], 0)
    count = lengths[0, owner]
    rows = 40
    slots = panel_ref.shape[2]
    q = lax.broadcasted_iota(jnp.int32, (rows, slots), 0)
    slot = lax.broadcasted_iota(jnp.int32, (rows, slots), 1)
    picks = []
    for e in range(4):
        base = 32 * (owner ^ e)
        wanted = jnp.where(q < 32, base + q, jnp.where(q == 32, base - 1, base + 32))
        inside = (q < 34) & (wanted >= 0) & (wanted < 128)
        local = wanted - start
        hit = inside & (local == slot) & (slot < count)
        picks.append(hit.astype(F32).astype(BF))
    pick = jnp.concatenate(picks, axis=0)
    scratch = outs[4]
    for i in range(UNIT):
        pair = jnp.concatenate([panel_ref[i], panel_ref[i + UNIT]], axis=0)
        got = lax.dot_general(
            pick, pair, (((1,), (1,)), ((), ())), preferred_element_type=F32
        )
        scratch[pl.ds(i, 4 * rows, stride=UNIT), :] = got
    seg_row = seg_ref[...].astype(F32) + 1.0
    for e in range(4):
        target = owner ^ e
        base = e * rows * UNIT
        if e == 0:
            scratch[pl.ds(base + 34 * UNIT, 1), :] = seg_row
        else:
            up = (target == owner + 1).astype(F32)
            down = (target == owner - 1).astype(F32)
            scratch[pl.ds(base + 35 * UNIT, 1), :] = seg_row * up
            scratch[pl.ds(base + 36 * UNIT, 1), :] = seg_row * down
    for e in range(4):
        outs[e][...] = scratch[pl.ds(e * rows * UNIT, rows * UNIT), :].astype(BF)


def select_panels(lengths, panels_t, seg):
    return pl.pallas_call(
        select_kernel,
        out_shape=[jax.ShapeDtypeStruct((640, 128), BF)] * 4,
        in_specs=[pl.BlockSpec(memory_space=pl.ANY)] * 3,
        out_specs=[WHOLE] * 4,
        scratch_shapes=[
            pltpu.VMEM((2560, 128), F32),
            pltpu.SMEM(lengths.shape, jnp.int32),
            pltpu.VMEM(panels_t.shape, BF),
            pltpu.VMEM(seg.shape, jnp.int32),
            pltpu.SemaphoreType.DMA((3,)),
        ],
        compiler_params=vmem(56),
        cost_estimate=cost(2 * 160 * 65 * 2048, 2 << 20),
    )(lengths, panels_t, seg)


def norm_kernel(
    a_ref, b_ref, wa_ref, wb_ref, kern_ref, gain_ref,
    ln_ref, normed_ref, rstd_ref, frames_ref, segs_ref, stack_ref,
    units, weight, segs, *blocks,
):
    step = pl.program_id(0)
    me = lax.axis_index("tensor")

    @pl.when(step == 0)
    def _():
        lane = lax.broadcasted_iota(jnp.int32, (256, 256), 0)
        out_lane = lax.broadcasted_iota(jnp.int32, (256, 256), 1)
        source = (out_lane // 64 % 2) * 128 + (out_lane // 128) * 64 + out_lane % 64
        swap = (lane == source).astype(F32).astype(BF)
        for d in range(4):
            weight[pl.ds(128 * d, 64), :] = wa_ref[d]
            weight[pl.ds(128 * d + 64, 64), :] = wb_ref[d]
            both = jnp.concatenate([a_ref[d, pl.ds(0, 544), :], b_ref[d, pl.ds(0, 544), :]], axis=1)
            mixed = jnp.dot(both, swap, preferred_element_type=F32).astype(BF)
            for p in range(34):
                at = p + 1 if p < 32 else (0 if p == 32 else 33)
                for half in range(2):
                    units[2 * at + half, :, pl.ds(128 * d, 128)] = mixed[
                        16 * p : 16 * p + 16, 128 * half : 128 * half + 128
                    ]
        eye = (
            lax.broadcasted_iota(jnp.int32, (128, 128), 0)
            == lax.broadcasted_iota(jnp.int32, (128, 128), 1)
        ).astype(F32)
        ones = jnp.ones((128, 128), BF)

        def column(ref, d, q):
            row = ref[d, pl.ds(q * UNIT, 16), :].astype(F32)[0:1]
            return jnp.dot((eye * row).astype(BF), ones, preferred_element_type=F32)

        for c in range(2):
            ref = (a_ref, b_ref)[c]
            for d in range(4):
                at = me ^ (ORDER[d] ^ c)
                segs[pl.ds(pl.multiple_of(HALO + 128 * at, 16), 128), :] = column(ref, d, 34)

                @pl.when(at == 7)
                def _():
                    segs[pl.ds(0, HALO), :] = column(ref, d, 35)[128 - HALO :]

                @pl.when(at == 0)
                def _():
                    segs[pl.ds(HALO + 1024, HALO), :] = column(ref, d, 36)[:HALO]

        for wide in (blocks[1], blocks[4]):
            wide[pl.ds(160, 96), :] = jnp.zeros((96, wide.shape[1]), BF)

    outs = (ln_ref, normed_ref, rstd_ref, segs_ref, stack_ref)
    for i in range(2):
        norm_block(me, 7 - 2 * step - i, kern_ref, gain_ref, units, weight, segs, *blocks[3 * i : 3 * i + 3], *outs)

    @pl.when(step == 3)
    def _():
        frames_ref[...] = blocks[4][pl.ds(0, 160), :].astype(F32)


def norm_block(
    me, at_step, kern_ref, gain_ref, units, weight, segs, near_segs, wide, near,
    ln_ref, normed_ref, rstd_ref, segs_ref, stack_ref,
):
    spot = lax.rem(at_step, 4)
    block = me ^ (2 * (spot ^ (spot // 2))) ^ (at_step // 4)
    rows = units[pl.ds(8 * block + 1, 10)].reshape(160, 512)
    wide[pl.ds(0, 160), :] = jnp.dot(rows, weight[...], preferred_element_type=F32).astype(BF)
    near_segs[...] = segs[pl.ds(pl.multiple_of(128 * block, 128), 160), :]

    stack_ref[...] = rows
    segs_ref[...] = near_segs[...]

    col = lax.broadcasted_iota(jnp.int32, (128, 256), 1) - lax.broadcasted_iota(jnp.int32, (128, 256), 0)
    here = near_segs[pl.ds(HALO, 128), :]
    shift = []
    for j in (0, 1, 3, 4):
        same = (near_segs[pl.ds(HALO - 2 + j, 128), :] == here).astype(F32)
        same = jnp.concatenate([same, same], axis=1)
        shift.append(jnp.where(col == HALO - 2 + j, same, 0.0).astype(BF))
    near[...] = jnp.dot(jnp.concatenate(shift, axis=0), wide[...], preferred_element_type=F32)

    taps = [kern_ref[pl.ds(j, 1), :] for j in range(5)]
    gain = gain_ref[...]
    for r in range(0, 128, 16):
        mixed = (1.0 + taps[2]) * wide[pl.ds(HALO + r, 16), :].astype(F32)
        for n, j in enumerate((0, 1, 3, 4)):
            mixed = mixed + taps[j] * near[pl.ds(128 * n + r, 16), :]
        mean = jnp.mean(mixed, axis=1, keepdims=True)
        center = mixed - mean
        rstd = lax.rsqrt(jnp.mean(center * center, axis=1, keepdims=True) + 1e-05)
        normed = center * rstd
        ln_ref[pl.ds(pl.multiple_of(128 * at_step + r, 16), 16), :] = (normed * gain).astype(BF)
        normed_ref[pl.ds(r, 16), :] = normed
        rstd_ref[pl.ds(r, 16), :] = jnp.broadcast_to(rstd, (16, 128))


def normalise(a, b, wa, wb, kern, gain):
    d_model = kern.shape[1]
    return pl.pallas_call(
        norm_kernel,
        grid=(4,),
        in_specs=[WHOLE] * 6,
        out_specs=[WHOLE] * 6,
        scratch_shapes=[
            pltpu.VMEM((68, 16, 512), BF),
            pltpu.VMEM((512, d_model), BF),
            pltpu.VMEM((1056, 128), F32),
        ]
        + [
            pltpu.VMEM((160, 128), F32),
            pltpu.VMEM((256, d_model), BF),
            pltpu.VMEM((512, d_model), F32),
        ]
        * 2,
        out_shape=[
            jax.ShapeDtypeStruct((1024, d_model), BF),
            jax.ShapeDtypeStruct((128, d_model), F32),
            jax.ShapeDtypeStruct((128, 128), F32),
            jax.ShapeDtypeStruct((160, d_model), F32),
            jax.ShapeDtypeStruct((160, 128), F32),
            jax.ShapeDtypeStruct((160, 512), BF),
        ],
        compiler_params=vmem(20),
        cost_estimate=cost(12 * 10**9, 10 << 20),
    )(a, b, wa, wb, kern, gain)


def hidden_kernel(ln_ref, up_ref, down_ref, hid_ref, slope_ref, ln_t_ref):
    del down_ref
    half = ln_ref.shape[0] // 2

    def block(r, carry):
        rows = pl.ds(pl.multiple_of(half * r, 128), half)
        for c in range(0, up_ref.shape[1], 256):
            part = pl.ds(c, 256)
            pre = jnp.dot(ln_ref[rows, :], up_ref[:, part], preferred_element_type=F32)
            sig = 1.0 / (1.0 + jnp.exp(-pre))
            hid_ref[r, part, :] = (pre * sig).astype(BF).T
            slope_ref[rows, part] = 0.5 * sig * (1.0 + pre * (1.0 - sig))
        for c in range(0, ln_ref.shape[1], 256):
            part = pl.ds(c, 256)
            ln_t_ref[r, part, :] = ln_ref[rows, part].T
        return carry

    lax.fori_loop(0, 2, block, 0)


def hidden_rows(ln, up, down):
    rows, d_model = ln.shape
    ff = up.shape[1]
    return pl.pallas_call(
        hidden_kernel,
        in_specs=[WHOLE] * 3,
        out_specs=[WHOLE] * 3,
        out_shape=[
            jax.ShapeDtypeStruct((2, ff, rows // 2), BF),
            jax.ShapeDtypeStruct((rows, ff), F32),
            jax.ShapeDtypeStruct((2, d_model, rows // 2), BF),
        ],
        compiler_params=vmem(12),
        cost_estimate=cost(2 * rows * d_model * ff, 10 << 20, rows * ff),
    )(ln, up, down)


def backward_kernel(side, cot_ref, slope_ref, up_ref, down_ref, dpre_ref, dln_ref):
    cols = (((1,), (1,)), ((), ()))
    rows = dln_ref.shape[0]
    grad = cot_ref[...].reshape(dln_ref.shape)
    for c in range(0, up_ref.shape[1], 256):
        part = pl.ds(c, 256)
        dhid = lax.dot_general(grad, down_ref[part, :], cols, preferred_element_type=F32)
        dpre_ref[:, part] = (dhid * slope_ref[pl.ds(rows * side, rows), part]).astype(BF)
    dln_ref[...] = lax.dot_general(
        dpre_ref[...], up_ref[...], cols, preferred_element_type=F32
    ).astype(BF)


def backward_rows(side, cot, slope, up, down):
    d_model, ff = up.shape
    half = slope.shape[0] // 2
    return pl.pallas_call(
        functools.partial(backward_kernel, side),
        in_specs=[WHOLE] * 4,
        out_specs=[WHOLE] * 2,
        out_shape=[jax.ShapeDtypeStruct((half, ff), BF), jax.ShapeDtypeStruct((half, d_model), BF)],
        compiler_params=vmem(12),
        cost_estimate=cost(4 * half * d_model * ff, 10 << 20),
    )(cot, slope, up, down)


PARTS = ((0, 1, 2, 3), (1, 0, 2, 3), (2, 3, 0, 1), (3, 2, 0, 1))
SPREAD = ((0, 1, 2, 3), (1, 2, 3, 0), (2, 3, 0, 1), (3, 0, 1, 2))
YZ = (("dp", 1), ("context", 1), ("dp", 3), ("context", 3))


def piece_code(y, z, r, axes):
    ry, rz = y ^ (r // 4), z ^ (r % 4)
    bits = ((ry & 1) ^ (ry >> 1), (rz & 1) ^ (rz >> 1), ry >> 1, rz >> 1)
    a, b, c, d = (bits[i] for i in axes)
    return (a << 3) | (b << 2) | (c << 1) | d


def weight_kernel(k, hid_ref, ca_ref, cb_ref, ln_ref, da_ref, db_ref, keep_ref, send_ref, both):
    y, z = lax.axis_index("dp"), lax.axis_index("context")
    half = hid_ref.shape[2]
    cols, wide, ff_cols = pl.ds(384 * k, 384), pl.ds(768 * (k // 2), 768), pl.ds(384 * (k % 2), 384)
    cot = [ref[:, :, cols].reshape(half, 384) for ref in (ca_ref, cb_ref)]
    down = jnp.dot(hid_ref[0], cot[0], preferred_element_type=F32)
    down += jnp.dot(hid_ref[1], cot[1], preferred_element_type=F32)
    down = (0.5 * down).astype(BF)
    up = jnp.dot(ln_ref[0, wide, :], da_ref[:, ff_cols], preferred_element_type=F32)
    up += jnp.dot(ln_ref[1, wide, :], db_ref[:, ff_cols], preferred_element_type=F32)
    up = up.astype(BF)
    for r in range(16):
        code = piece_code(y, z, r, PARTS[k])
        both[code, pl.ds(0, 48), :] = down[48 * r : 48 * r + 48]
        both[code, pl.ds(48, 48), :] = up[48 * r : 48 * r + 48]
    keep_ref[...] = both[pl.ds(0, 8)]
    send_ref[...] = both[pl.ds(8, 8)]


def weight_part(k, hidden, ca, cb, ln, dpre_a, dpre_b):
    rows = 2 * hidden.shape[2]
    return pl.pallas_call(
        functools.partial(weight_kernel, k),
        in_specs=[WHOLE] * 6,
        out_specs=[WHOLE] * 2,
        out_shape=[jax.ShapeDtypeStruct((8, 96, 384), BF)] * 2,
        scratch_shapes=[pltpu.VMEM((16, 96, 384), BF)],
        compiler_params=vmem(14),
        cost_estimate=cost(4 * rows * 768 * 384, 7 << 20),
    )(hidden, ca, cb, ln, dpre_a, dpre_b)


def piece_row(y, z, code, axes):
    bits = [0] * 4
    for i, axis in enumerate(axes):
        bits[axis] = (code >> (3 - i)) & 1
    ay, az, by, bz = bits
    return 4 * (y ^ (2 * by | (ay ^ by))) + (z ^ (2 * bz | (az ^ bz)))


def place_pieces(side, bufs, down_ref, up_ref, stage, sems):
    y, z = lax.axis_index("dp"), lax.axis_index("context")
    copies = []
    for k in range(4):
        for c in range(8):
            row = 48 * piece_row(y, z, 8 * side + c, SPREAD[k])
            for i, (out, row0, col0) in enumerate(((down_ref, 0, 384 * k), (up_ref, 768 * (k // 2), 384 * (k % 2)))):
                stage[k, c, i] = bufs[k][pl.ds(96 * c + 48 * i, 48), :].astype(F32)
                to = out.at[pl.ds(pl.multiple_of(row0 + row, 16), 48), pl.ds(col0, 384)]
                copies.append(pltpu.make_async_copy(stage.at[k, c, i], to, sems.at[k, c, i]))
                copies[-1].start()
    return copies


def place_own_kernel(*refs):
    for copy in place_pieces(0, refs[:4], *refs[4:]):
        copy.wait()


def place_rest_kernel(*refs):
    own, rec = refs[:4], refs[4:8]
    down_ref, up_ref, *small_out = refs[10:15]
    stage, sems, front_ref, kern_ref, gain_ref, small_sems = refs[15:]
    for k in range(4):
        last = [ref[pl.ds(768, 80), :].astype(F32) for ref in (own[k], rec[k])]
        cols = pl.ds(384 * k, 384)
        front_ref[:, cols] = last[0][:64] + last[1][:64]
        small = (last[0][64:72] + last[0][72:]) + (last[1][64:72] + last[1][72:])
        kern_ref[:, cols] = small[:5]
        gain_ref[cols] = small[5]
    copies = [
        pltpu.make_async_copy(src, dst, small_sems.at[i])
        for i, (src, dst) in enumerate(zip((front_ref, kern_ref, gain_ref), small_out))
    ]
    for copy in copies:
        copy.start()
    for copy in copies + place_pieces(1, rec, down_ref, up_ref, stage, sems):
        copy.wait()


def place(own, rec):
    big = [jax.ShapeDtypeStruct((768, 1536), F32), jax.ShapeDtypeStruct((1536, 768), F32)]
    hbm = pl.BlockSpec(memory_space=pl.ANY)
    small = [(64, 1536), (5, 1536), (1536,)]
    scratch = [pltpu.VMEM((4, 8, 2, 48, 384), F32), pltpu.SemaphoreType.DMA((4, 8, 2))]
    started = pl.pallas_call(
        place_own_kernel,
        in_specs=[WHOLE] * 4,
        out_specs=[hbm] * 2,
        out_shape=big,
        scratch_shapes=scratch,
        compiler_params=vmem(40),
        cost_estimate=cost(1 << 20, 7 << 20),
    )(*own)
    return pl.pallas_call(
        place_rest_kernel,
        in_specs=[WHOLE] * 8 + [hbm] * 2,
        out_specs=[hbm] * 5,
        out_shape=big + [jax.ShapeDtypeStruct(shape, F32) for shape in small],
        input_output_aliases={8: 0, 9: 1},
        scratch_shapes=scratch
        + [pltpu.VMEM(shape, F32) for shape in small]
        + [pltpu.SemaphoreType.DMA((3,))],
        compiler_params=vmem(40),
        cost_estimate=cost(1 << 20, 7 << 20),
    )(*own, *rec, *started)


def high_low(value):
    high = value.astype(BF).astype(F32)
    return jnp.concatenate([high, value - high], axis=0).astype(BF)


def add_small(one, two):
    one, two = one.astype(F32), two.astype(F32)
    return high_low((one[:8] + one[8:]) + (two[:8] + two[8:]))


def tail_kernel(
    dln_ref, rec_ref, normed_ref, rstd_ref, frames_ref, segs_ref, stack_ref, cot_ref, kern_ref, gain_ref,
    keep_ref, send_ref, scaled, moved, sums,
):
    sums[...] = jnp.zeros_like(sums)
    taps = [kern_ref[pl.ds(j, 1), :] for j in range(5)]
    gain = gain_ref[...]
    wide_stack = stack_ref[...].astype(F32)
    for j in range(5):
        here = segs_ref[pl.ds(HALO, 128), :]
        same = (segs_ref[pl.ds(HALO - 2 + j, 128), :] == here).astype(F32)
        same = jnp.concatenate([same] * 4, axis=1)
        moved[pl.ds(128 * j, 128), :] = (same * wide_stack[HALO - 2 + j : HALO + 126 + j]).astype(BF)

    def fold(x):
        return x[0:8] + x[8:16]

    for r in range(0, 128, 16):
        at = pl.ds(r, 16)
        dln = dln_ref[at, :] + rec_ref[at, :].astype(F32)
        normed = normed_ref[at, :]
        rstd = rstd_ref[at, :][:, 0:1]
        sums[5] += fold(dln * normed)
        dnorm = dln * gain
        m1 = jnp.mean(dnorm, axis=1, keepdims=True)
        m2 = jnp.mean(dnorm * normed, axis=1, keepdims=True)
        dmixed = cot_ref[at, :].astype(F32) + rstd * (dnorm - m1 - normed * m2)
        dmixed = dmixed.astype(BF).astype(F32)
        here = segs_ref[pl.ds(HALO + r, 16), :]
        for j in range(5):
            near = frames_ref[pl.ds(HALO - 2 + r + j, 16), :]
            tap = taps[j]
            if j == 2:
                tap = tap + 1.0
                sums[j] += fold(dmixed * near)
            else:
                same = (segs_ref[pl.ds(HALO - 2 + r + j, 16), :] == here).astype(F32)
                same = jnp.concatenate([same] * 12, axis=1)
                sums[j] += fold(dmixed * (same * near))
            scaled[pl.ds(128 * j + r, 16), :] = (tap * dmixed).astype(BF)

    front = lax.dot_general(
        moved[...], scaled[...], (((0,), (0,)), ((), ())), preferred_element_type=F32
    )
    for d in range(4):
        keep_ref[pl.ds(64 * d, 64), :] = front[128 * d : 128 * d + 64]
        send_ref[pl.ds(64 * d, 64), :] = front[128 * d + 64 : 128 * d + 128].astype(BF)
    small = jnp.concatenate(
        [jnp.sum(sums[j], axis=0, keepdims=True) for j in range(6)] + [jnp.zeros((2, 1536), F32)], axis=0
    )
    small = high_low(small)
    keep_ref[pl.ds(256, 16), :] = small.astype(F32)
    send_ref[pl.ds(256, 16), :] = small


def tail(pieces, normed, rstd, frames, segs, stack, cot, kern, gain):
    args = (*pieces, normed, rstd, frames, segs, stack, cot, kern, gain)
    return pl.pallas_call(
        tail_kernel,
        in_specs=[WHOLE] * len(args),
        out_specs=[WHOLE] * 2,
        out_shape=[jax.ShapeDtypeStruct((272, 1536), F32), jax.ShapeDtypeStruct((272, 1536), BF)],
        scratch_shapes=[
            pltpu.VMEM((640, 1536), BF), pltpu.VMEM((640, 512), BF), pltpu.VMEM((6, 8, 1536), F32),
        ],
        compiler_params=vmem(16),
        cost_estimate=cost(60 * 10**9, 6 << 20),
    )(*args)


def gather_core(value):
    own = jnp.stack([value] + [xor_send(value, "tensor", m, 8) for m in ORDER[1:]])
    return own, xor_send(own, "tensor", 1, 8)


def after(value, *others):
    return lax.optimization_barrier((value, *others))[0]


def over(axis, value):
    return xor_send(value, *YZ[axis], 4)


def glue(kernel, outs, *args, flops=5 * 10**8):
    return pl.pallas_call(
        kernel,
        in_specs=[WHOLE] * len(args),
        out_specs=[WHOLE] * len(outs),
        out_shape=[jax.ShapeDtypeStruct(*out) for out in outs],
        compiler_params=vmem(16),
        cost_estimate=cost(flops, 1 << 16),
    )(*args)


def sum_kernel(one, two, three, four, out):
    out[...] = (one[...] + two[...]) + (three[...] + four[...])


def dln_core_kernel(own, rec, keep, send):
    for i in range(4):
        at, to = pl.ds(128 * i, 128), pl.ds(128 * (i // 2), 128)
        total = own[at, :].astype(F32) + rec[at, :].astype(F32)
        if i % 2:
            send[to, :] = total.astype(BF)
        else:
            keep[to, :] = total


def halve_kernel(own, rec, keep, send):
    n = keep.shape[0]
    keep[...] = own[pl.ds(0, n)] + rec[pl.ds(0, n)].astype(F32)
    send[...] = (own[pl.ds(n, n)] + rec[pl.ds(n, n)].astype(F32)).astype(BF)


def halve_first_kernel(own, rec, keep, send):
    n = keep.shape[0]
    keep[...] = own[pl.ds(0, n)].astype(F32) + rec[pl.ds(0, n)].astype(F32)
    send[...] = (own[pl.ds(n, n)].astype(F32) + rec[pl.ds(n, n)].astype(F32)).astype(BF)


def join_kernel(own0, rec0, own1, rec1, keep, send):
    for i, (own, rec) in enumerate(((own0, rec0), (own1, rec1))):
        total = own[...] + rec[...].astype(F32)
        keep[:, pl.ds(96 * i, 96), :] = total[:2]
        send[:, pl.ds(96 * i, 96), :] = total[2:].astype(BF)


def front_core_kernel(own, rec, keep0, keep1, send0, send1):
    for i in range(4):
        at = pl.ds(64 * i, 64)
        total = own[at, :] + rec[at, :].astype(F32)
        out = send0 if i % 2 else keep0
        out[pl.ds(64 * (i // 2), 64), :] = total[:, :768].astype(out.dtype)
        out = send1 if i // 2 else keep1
        out[pl.ds(64 * (i % 2), 64), :] = total[:, 768:].astype(out.dtype)
    small = add_small(own[pl.ds(256, 16), :], rec[pl.ds(256, 16), :])
    for i, (keep, send) in enumerate(((keep0, send0), (keep1, send1))):
        half = small[:, 768 * i : 768 * i + 768]
        keep[pl.ds(128, 16), :] = half.astype(F32)
        send[pl.ds(128, 16), :] = half


def front_x_kernel(own, rec, keep, send):
    keep[pl.ds(0, 64), :] = own[pl.ds(0, 64), :] + rec[pl.ds(0, 64), :].astype(F32)
    send[pl.ds(0, 64), :] = (own[pl.ds(64, 64), :] + rec[pl.ds(64, 64), :].astype(F32)).astype(BF)
    small = add_small(own[pl.ds(128, 16), :], rec[pl.ds(128, 16), :])
    keep[pl.ds(64, 16), :] = small.astype(F32)
    send[pl.ds(64, 16), :] = small


def spread_first_kernel(own, rec, front, front_rec, out0, out1):
    piece = (own[0] + rec[0].astype(F32)).astype(BF)
    front_rows = (front[pl.ds(0, 64), :] + front_rec[pl.ds(0, 64), :].astype(F32)).astype(BF)
    small = add_small(front[pl.ds(64, 16), :], front_rec[pl.ds(64, 16), :])
    for i, out in enumerate((out0, out1)):
        out[pl.ds(0, 96), :] = piece[96 * i : 96 * i + 96]
        cols = slice(384 * i, 384 * i + 384)
        out[pl.ds(96, 64), :] = front_rows[:, cols]
        out[pl.ds(160, 16), :] = small[:, cols]


def spread_kernel(own, rec, out):
    n = own.shape[0] - 80
    out[pl.ds(0, n), :] = own[pl.ds(0, n), :]
    out[pl.ds(n, n), :] = rec[pl.ds(0, n), :]
    out[pl.ds(2 * n, 64), :] = (own[pl.ds(n, 64), :].astype(F32) + rec[pl.ds(n, 64), :].astype(F32)).astype(BF)
    out[pl.ds(2 * n + 64, 16), :] = add_small(own[pl.ds(n + 64, 16), :], rec[pl.ds(n + 64, 16), :])


def halve_first(keep, rec):
    return glue(halve_first_kernel, [((4, 96, 384), F32), ((4, 96, 384), BF)], keep, rec)


def join_parts(k, pairs, recs):
    return glue(
        join_kernel, [((2, 192, 384), F32), ((2, 192, 384), BF)],
        pairs[k][0], recs[0], pairs[k + 1][0], recs[1],
    )


def reduce_ends(k, keep, send):
    keep, send = glue(
        halve_kernel, [((1, 192, 384), F32), ((1, 192, 384), BF)], keep, over(PARTS[k][2], send)
    )
    return keep, over(PARTS[k][3], send)


def spread_parts(ends, fronts):
    bufs = []
    for k in (0, 1):
        bufs += glue(spread_first_kernel, [((176, 384), BF)] * 2, *ends[k], *fronts[k])
    for s in (3, 2, 1):
        recs = [over(SPREAD[k][s], bufs[k]) for k in range(4)]
        rows = 2 * bufs[0].shape[0] - 80
        bufs = [glue(spread_kernel, [((rows, 384), BF)], bufs[k], recs[k])[0] for k in range(4)]
    return bufs, [over(SPREAD[k][0], bufs[k]) for k in range(4)]


def per_device(
    panels, lengths, segments, front_weight, conv_kernel, gain, up_weight, down_weight, cotangent
):
    gain_row = gain[None, :]
    cot = cotangent[0]

    picked = select_panels(lengths, jnp.transpose(panels[0, 0], (1, 2, 0)), segments)
    front_weight = after(front_weight, picked[0])
    got = [xor_send(picked[e], "context", e, 4) for e in (2, 1, 3)]
    wa, wb = gather_core(front_weight)
    (block,) = glue(sum_kernel, [((640, 128), BF)], picked[0], *got)
    cot_later = after(cot, block)
    pa, pb = gather_core(block)
    others = [xor_send(cot_later, "tensor", m ^ 1, 8) for m in ORDER]

    ln, normed, rstd, frames, segs, stack = normalise(pa, pb, wa, wb, conv_kernel, gain_row)
    hidden, slope, ln_t = hidden_rows(ln, up_weight, down_weight)
    slope, *others = lax.optimization_barrier((slope, *others))
    cb = jnp.stack(others)
    ca = xor_send(cb, "tensor", 1, 8)
    dpre_a, dln_keep = backward_rows(0, ca, slope, up_weight, down_weight)
    dpre_b, dln_send = backward_rows(1, cb, slope, up_weight, down_weight)

    dln_rec = xor_send(dln_send, "tensor", 1, 8)
    keep, send = glue(
        dln_core_kernel, [((256, 1536), F32), ((256, 1536), BF)], dln_keep, dln_rec
    )
    rec = xor_send(send, "tensor", 2, 8)
    parts = [weight_part(k, hidden, ca, cb, ln_t, dpre_a, dpre_b) for k in range(4)]
    firsts = [over(PARTS[k][0], parts[k][1]) for k in range(4)]
    pairs = [halve_first(parts[0][0], firsts[0])]
    rec = after(rec, pairs[0][1], *[p[0] for p in parts[1:]])
    keep, send = glue(halve_kernel, [((128, 1536), F32), ((128, 1536), BF)], keep, rec)
    pairs.append(halve_first(parts[1][0], firsts[1]))
    send = after(send, pairs[1][1])
    rec = xor_send(send, "tensor", 6, 8)
    pairs += [halve_first(parts[k][0], firsts[k]) for k in (2, 3)]
    seconds = [over(PARTS[k][1], pairs[k][1]) for k in range(4)]
    joined = join_parts(0, pairs, seconds[:2])
    pieces = (keep, after(rec, joined[1], *seconds[2:]))
    keep, send = tail(pieces, normed, rstd, frames, segs, stack, cot, conv_kernel, gain_row)
    ends = reduce_ends(0, *joined), reduce_ends(2, *join_parts(2, pairs, seconds[2:]))
    k0, k1, s0, s1 = glue(
        front_core_kernel, [((144, 768), F32)] * 2 + [((144, 768), BF)] * 2,
        keep, xor_send(send, "tensor", 1, 8), flops=FIRST,
    )
    half = [((80, 768), F32), ((80, 768), BF)]
    k0, s0 = glue(front_x_kernel, half, k0, xor_send(s0, "tensor", 2, 8), flops=FIRST)
    k1, s1 = glue(front_x_kernel, half, k1, xor_send(s1, "tensor", 6, 8), flops=FIRST)
    fronts = (k0, xor_send(s0, "tensor", 6, 8)), (k1, xor_send(s1, "tensor", 2, 8))
    own, rec = spread_parts(ends, fronts)
    grad_down, grad_up, grad_front, grad_kernel, grad_gain = place(own, rec)
    return (grad_front, grad_kernel, grad_gain, grad_up, grad_down)


def solution(mesh):
    return jax.shard_map(
        per_device,
        mesh=mesh,
        in_specs=(
            P("dp", "context", None, None, "tensor"),
            P("dp", None),
            P("dp", ("context", "tensor")),
            P("tensor", None),
            P(),
            P(),
            P(None, "tensor"),
            P("tensor", None),
            P("dp", ("context", "tensor"), None),
        ),
        out_specs=(P("tensor", None), P(), P(), P(None, "tensor"), P("tensor", None)),
        check_vma=False,
    )
```

```python
import functools

import jax
import jax.numpy as jnp
from jax import lax
from jax.experimental import pallas as pl
from jax.experimental.pallas import tpu as pltpu
from jax.sharding import PartitionSpec as P

BF = jnp.bfloat16
F32 = jnp.float32
ORDER = (0, 2, 6, 4)
XOR3 = (1, 3, 2)
UNIT = 16
HALO = 16
FIRST = 5 * 10**8


def vmem(limit):
    return pltpu.CompilerParams(vmem_limit_bytes=limit << 20)


def cost(flops, nbytes, trans=0):
    return pl.CostEstimate(flops=flops, bytes_accessed=nbytes, transcendentals=trans)


def full(shape):
    return pl.BlockSpec(shape, lambda *_: (0,) * len(shape))


WHOLE = pl.BlockSpec(memory_space=pltpu.VMEM)


def xor_send(value, axis, mask, size):
    return lax.ppermute(value, axis, [(i, i ^ mask) for i in range(size)])


def select_kernel(lengths_hbm, panel_hbm, seg_hbm, *outs):
    lengths, panel_ref, seg_ref, sem = outs[5:]
    copies = [
        pltpu.make_async_copy(src, dst, sem.at[i])
        for i, (src, dst) in enumerate(((panel_hbm, panel_ref), (seg_hbm, seg_ref), (lengths_hbm, lengths)))
    ]
    for copy in copies:
        copy.start()
    for copy in copies:
        copy.wait()
    owner = lax.axis_index("context")
    start = jnp.int32(0)
    for shard in range(3):
        start += jnp.where(shard < owner, lengths[0, shard], 0)
    count = lengths[0, owner]
    rows = 40
    slots = panel_ref.shape[2]
    q = lax.broadcasted_iota(jnp.int32, (rows, slots), 0)
    slot = lax.broadcasted_iota(jnp.int32, (rows, slots), 1)
    picks = []
    for e in range(4):
        base = 32 * (owner ^ e)
        wanted = jnp.where(q < 32, base + q, jnp.where(q == 32, base - 1, base + 32))
        inside = (q < 34) & (wanted >= 0) & (wanted < 128)
        local = wanted - start
        hit = inside & (local == slot) & (slot < count)
        picks.append(hit.astype(F32).astype(BF))
    pick = jnp.concatenate(picks, axis=0)
    scratch = outs[4]
    for i in range(UNIT):
        pair = jnp.concatenate([panel_ref[i], panel_ref[i + UNIT]], axis=0)
        got = lax.dot_general(
            pick, pair, (((1,), (1,)), ((), ())), preferred_element_type=F32
        )
        scratch[pl.ds(i, 4 * rows, stride=UNIT), :] = got
    seg_row = seg_ref[...].astype(F32) + 1.0
    for e in range(4):
        target = owner ^ e
        base = e * rows * UNIT
        if e == 0:
            scratch[pl.ds(base + 34 * UNIT, 1), :] = seg_row
        else:
            up = (target == owner + 1).astype(F32)
            down = (target == owner - 1).astype(F32)
            scratch[pl.ds(base + 35 * UNIT, 1), :] = seg_row * up
            scratch[pl.ds(base + 36 * UNIT, 1), :] = seg_row * down
    for e in range(4):
        outs[e][...] = scratch[pl.ds(e * rows * UNIT, rows * UNIT), :].astype(BF)


def select_panels(lengths, panels_t, seg):
    return pl.pallas_call(
        select_kernel,
        out_shape=[jax.ShapeDtypeStruct((640, 128), BF)] * 4,
        in_specs=[pl.BlockSpec(memory_space=pl.ANY)] * 3,
        out_specs=[WHOLE] * 4,
        scratch_shapes=[
            pltpu.VMEM((2560, 128), F32),
            pltpu.SMEM(lengths.shape, jnp.int32),
            pltpu.VMEM(panels_t.shape, BF),
            pltpu.VMEM(seg.shape, jnp.int32),
            pltpu.SemaphoreType.DMA((3,)),
        ],
        compiler_params=vmem(56),
        cost_estimate=cost(2 * 160 * 65 * 2048, 2 << 20),
    )(lengths, panels_t, seg)


def norm_kernel(
    a_ref, b_ref, wa_ref, wb_ref, kern_ref, gain_ref,
    ln_ref, normed_ref, rstd_ref, frames_ref, segs_ref, stack_ref,
    units, weight, segs, *blocks,
):
    step = pl.program_id(0)
    me = lax.axis_index("tensor")

    @pl.when(step == 0)
    def _():
        lane = lax.broadcasted_iota(jnp.int32, (256, 256), 0)
        out_lane = lax.broadcasted_iota(jnp.int32, (256, 256), 1)
        source = (out_lane // 64 % 2) * 128 + (out_lane // 128) * 64 + out_lane % 64
        swap = (lane == source).astype(F32).astype(BF)
        for d in range(4):
            weight[pl.ds(128 * d, 64), :] = wa_ref[d]
            weight[pl.ds(128 * d + 64, 64), :] = wb_ref[d]
            both = jnp.concatenate([a_ref[d, pl.ds(0, 544), :], b_ref[d, pl.ds(0, 544), :]], axis=1)
            mixed = jnp.dot(both, swap, preferred_element_type=F32).astype(BF)
            for p in range(34):
                at = p + 1 if p < 32 else (0 if p == 32 else 33)
                for half in range(2):
                    units[2 * at + half, :, pl.ds(128 * d, 128)] = mixed[
                        16 * p : 16 * p + 16, 128 * half : 128 * half + 128
                    ]
        eye = (
            lax.broadcasted_iota(jnp.int32, (128, 128), 0)
            == lax.broadcasted_iota(jnp.int32, (128, 128), 1)
        ).astype(F32)
        ones = jnp.ones((128, 128), BF)

        def column(ref, d, q):
            row = ref[d, pl.ds(q * UNIT, 16), :].astype(F32)[0:1]
            return jnp.dot((eye * row).astype(BF), ones, preferred_element_type=F32)

        for c in range(2):
            ref = (a_ref, b_ref)[c]
            for d in range(4):
                at = me ^ (ORDER[d] ^ c)
                segs[pl.ds(pl.multiple_of(HALO + 128 * at, 16), 128), :] = column(ref, d, 34)

                @pl.when(at == 7)
                def _():
                    segs[pl.ds(0, HALO), :] = column(ref, d, 35)[128 - HALO :]

                @pl.when(at == 0)
                def _():
                    segs[pl.ds(HALO + 1024, HALO), :] = column(ref, d, 36)[:HALO]

        for wide in (blocks[1], blocks[4]):
            wide[pl.ds(160, 96), :] = jnp.zeros((96, wide.shape[1]), BF)

    outs = (ln_ref, normed_ref, rstd_ref, segs_ref, stack_ref)
    for i in range(2):
        norm_block(me, 7 - 2 * step - i, kern_ref, gain_ref, units, weight, segs, *blocks[3 * i : 3 * i + 3], *outs)

    @pl.when(step == 3)
    def _():
        frames_ref[...] = blocks[4][pl.ds(0, 160), :].astype(F32)


def norm_block(
    me, at_step, kern_ref, gain_ref, units, weight, segs, near_segs, wide, near,
    ln_ref, normed_ref, rstd_ref, segs_ref, stack_ref,
):
    spot = lax.rem(at_step, 4)
    block = me ^ (2 * (spot ^ (spot // 2))) ^ (at_step // 4)
    rows = units[pl.ds(8 * block + 1, 10)].reshape(160, 512)
    wide[pl.ds(0, 160), :] = jnp.dot(rows, weight[...], preferred_element_type=F32).astype(BF)
    near_segs[...] = segs[pl.ds(pl.multiple_of(128 * block, 128), 160), :]

    stack_ref[...] = rows
    segs_ref[...] = near_segs[...]

    col = lax.broadcasted_iota(jnp.int32, (128, 256), 1) - lax.broadcasted_iota(jnp.int32, (128, 256), 0)
    here = near_segs[pl.ds(HALO, 128), :]
    shift = []
    for j in (0, 1, 3, 4):
        same = (near_segs[pl.ds(HALO - 2 + j, 128), :] == here).astype(F32)
        same = jnp.concatenate([same, same], axis=1)
        shift.append(jnp.where(col == HALO - 2 + j, same, 0.0).astype(BF))
    near[...] = jnp.dot(jnp.concatenate(shift, axis=0), wide[...], preferred_element_type=F32)

    taps = [kern_ref[pl.ds(j, 1), :] for j in range(5)]
    gain = gain_ref[...]
    for r in range(0, 128, 16):
        mixed = (1.0 + taps[2]) * wide[pl.ds(HALO + r, 16), :].astype(F32)
        for n, j in enumerate((0, 1, 3, 4)):
            mixed = mixed + taps[j] * near[pl.ds(128 * n + r, 16), :]
        mean = jnp.mean(mixed, axis=1, keepdims=True)
        center = mixed - mean
        rstd = lax.rsqrt(jnp.mean(center * center, axis=1, keepdims=True) + 1e-05)
        normed = center * rstd
        ln_ref[pl.ds(pl.multiple_of(128 * at_step + r, 16), 16), :] = (normed * gain).astype(BF)
        normed_ref[pl.ds(r, 16), :] = normed
        rstd_ref[pl.ds(r, 16), :] = jnp.broadcast_to(rstd, (16, 128))


def normalise(a, b, wa, wb, kern, gain):
    d_model = kern.shape[1]
    return pl.pallas_call(
        norm_kernel,
        grid=(4,),
        in_specs=[WHOLE] * 6,
        out_specs=[WHOLE] * 6,
        scratch_shapes=[
            pltpu.VMEM((68, 16, 512), BF),
            pltpu.VMEM((512, d_model), BF),
            pltpu.VMEM((1056, 128), F32),
        ]
        + [
            pltpu.VMEM((160, 128), F32),
            pltpu.VMEM((256, d_model), BF),
            pltpu.VMEM((512, d_model), F32),
        ]
        * 2,
        out_shape=[
            jax.ShapeDtypeStruct((1024, d_model), BF),
            jax.ShapeDtypeStruct((128, d_model), F32),
            jax.ShapeDtypeStruct((128, 128), F32),
            jax.ShapeDtypeStruct((160, d_model), F32),
            jax.ShapeDtypeStruct((160, 128), F32),
            jax.ShapeDtypeStruct((160, 512), BF),
        ],
        compiler_params=vmem(20),
        cost_estimate=cost(12 * 10**9, 10 << 20),
    )(a, b, wa, wb, kern, gain)


def hidden_kernel(ln_ref, up_ref, down_ref, hid_ref, slope_ref, ln_t_ref):
    del down_ref
    half = ln_ref.shape[0] // 2

    def block(r, carry):
        rows = pl.ds(pl.multiple_of(half * r, 128), half)
        for c in range(0, up_ref.shape[1], 256):
            part = pl.ds(c, 256)
            pre = jnp.dot(ln_ref[rows, :], up_ref[:, part], preferred_element_type=F32)
            sig = 1.0 / (1.0 + jnp.exp(-pre))
            hid_ref[r, part, :] = (pre * sig).astype(BF).T
            slope_ref[rows, part] = 0.5 * sig * (1.0 + pre * (1.0 - sig))
        for c in range(0, ln_ref.shape[1], 256):
            part = pl.ds(c, 256)
            ln_t_ref[r, part, :] = ln_ref[rows, part].T
        return carry

    lax.fori_loop(0, 2, block, 0)


def hidden_rows(ln, up, down):
    rows, d_model = ln.shape
    ff = up.shape[1]
    return pl.pallas_call(
        hidden_kernel,
        in_specs=[WHOLE] * 3,
        out_specs=[WHOLE] * 3,
        out_shape=[
            jax.ShapeDtypeStruct((2, ff, rows // 2), BF),
            jax.ShapeDtypeStruct((rows, ff), F32),
            jax.ShapeDtypeStruct((2, d_model, rows // 2), BF),
        ],
        compiler_params=vmem(12),
        cost_estimate=cost(2 * rows * d_model * ff, 10 << 20, rows * ff),
    )(ln, up, down)


def backward_kernel(side, cot_ref, slope_ref, up_ref, down_ref, dpre_ref, dln_ref):
    cols = (((1,), (1,)), ((), ()))
    rows = dln_ref.shape[0]
    grad = cot_ref[...].reshape(dln_ref.shape)
    for c in range(0, up_ref.shape[1], 256):
        part = pl.ds(c, 256)
        dhid = lax.dot_general(grad, down_ref[part, :], cols, preferred_element_type=F32)
        dpre_ref[:, part] = (dhid * slope_ref[pl.ds(rows * side, rows), part]).astype(BF)
    dln_ref[...] = lax.dot_general(
        dpre_ref[...], up_ref[...], cols, preferred_element_type=F32
    ).astype(BF)


def backward_rows(side, cot, slope, up, down):
    d_model, ff = up.shape
    half = slope.shape[0] // 2
    return pl.pallas_call(
        functools.partial(backward_kernel, side),
        in_specs=[WHOLE] * 4,
        out_specs=[WHOLE] * 2,
        out_shape=[jax.ShapeDtypeStruct((half, ff), BF), jax.ShapeDtypeStruct((half, d_model), BF)],
        compiler_params=vmem(12),
        cost_estimate=cost(4 * half * d_model * ff, 10 << 20),
    )(cot, slope, up, down)


PARTS = ((0, 1, 2, 3), (1, 0, 2, 3), (2, 3, 0, 1), (3, 2, 0, 1))
SPREAD = ((0, 1, 2, 3), (1, 2, 3, 0), (2, 3, 0, 1), (3, 0, 1, 2))
YZ = (("dp", 1), ("context", 1), ("dp", 3), ("context", 3))


def piece_code(y, z, r, axes):
    ry, rz = y ^ (r // 4), z ^ (r % 4)
    bits = ((ry & 1) ^ (ry >> 1), (rz & 1) ^ (rz >> 1), ry >> 1, rz >> 1)
    a, b, c, d = (bits[i] for i in axes)
    return (a << 3) | (b << 2) | (c << 1) | d


def weight_kernel(k, hid_ref, ca_ref, cb_ref, ln_ref, da_ref, db_ref, keep_ref, send_ref):
    y, z = lax.axis_index("dp"), lax.axis_index("context")
    half = hid_ref.shape[2]
    cols, wide, ff_cols = pl.ds(384 * k, 384), pl.ds(768 * (k // 2), 768), pl.ds(384 * (k % 2), 384)
    cot = [ref[:, :, cols].reshape(half, 384) for ref in (ca_ref, cb_ref)]
    down = jnp.dot(hid_ref[0], cot[0], preferred_element_type=F32)
    down += jnp.dot(hid_ref[1], cot[1], preferred_element_type=F32)
    down = (0.5 * down).astype(BF)
    up = jnp.dot(ln_ref[0, wide, :], da_ref[:, ff_cols], preferred_element_type=F32)
    up += jnp.dot(ln_ref[1, wide, :], db_ref[:, ff_cols], preferred_element_type=F32)
    up = up.astype(BF)
    flip = (4, 1, 12, 3)[PARTS[k][0]]
    for r in range(16):
        if r > r ^ flip:
            continue
        code = piece_code(y, z, r, PARTS[k])
        mine, low = code < 8, code & 7
        for at, value in ((0, down), (48, up)):
            one = value[48 * r : 48 * r + 48]
            two = value[48 * (r ^ flip) : 48 * (r ^ flip) + 48]
            keep_ref[low, pl.ds(at, 48), :] = lax.select(mine, one, two)
            send_ref[low, pl.ds(at, 48), :] = lax.select(mine, two, one)


def weight_part(k, hidden, ca, cb, ln, dpre_a, dpre_b):
    rows = 2 * hidden.shape[2]
    return pl.pallas_call(
        functools.partial(weight_kernel, k),
        in_specs=[WHOLE] * 6,
        out_specs=[WHOLE] * 2,
        out_shape=[jax.ShapeDtypeStruct((8, 96, 384), BF)] * 2,
        compiler_params=vmem(14),
        cost_estimate=cost(4 * rows * 768 * 384, 7 << 20),
    )(hidden, ca, cb, ln, dpre_a, dpre_b)


def piece_row(y, z, code, axes):
    bits = [0] * 4
    for i, axis in enumerate(axes):
        bits[axis] = (code >> (3 - i)) & 1
    ay, az, by, bz = bits
    return 4 * (y ^ (2 * by | (ay ^ by))) + (z ^ (2 * bz | (az ^ bz)))


def place_pieces(side, bufs, down_ref, up_ref, stage, sems):
    y, z = lax.axis_index("dp"), lax.axis_index("context")
    copies = []
    for k in range(4):
        for c in range(8):
            row = 48 * piece_row(y, z, 8 * side + c, SPREAD[k])
            for i, (out, row0, col0) in enumerate(((down_ref, 0, 384 * k), (up_ref, 768 * (k // 2), 384 * (k % 2)))):
                stage[k, c, i] = bufs[k][pl.ds(96 * c + 48 * i, 48), :].astype(F32)
                to = out.at[pl.ds(pl.multiple_of(row0 + row, 16), 48), pl.ds(col0, 384)]
                copies.append(pltpu.make_async_copy(stage.at[k, c, i], to, sems.at[k, c, i]))
                copies[-1].start()
    return copies


def place_own_kernel(*refs):
    for copy in place_pieces(0, refs[:4], *refs[4:]):
        copy.wait()


def place_rest_kernel(*refs):
    own, rec = refs[:4], refs[4:8]
    down_ref, up_ref, *small_out = refs[10:15]
    stage, sems, front_ref, kern_ref, gain_ref, small_sems = refs[15:]
    for k in range(4):
        last = [ref[pl.ds(768, 80), :].astype(F32) for ref in (own[k], rec[k])]
        cols = pl.ds(384 * k, 384)
        front_ref[:, cols] = last[0][:64] + last[1][:64]
        small = (last[0][64:72] + last[0][72:]) + (last[1][64:72] + last[1][72:])
        kern_ref[:, cols] = small[:5]
        gain_ref[cols] = small[5]
    copies = [
        pltpu.make_async_copy(src, dst, small_sems.at[i])
        for i, (src, dst) in enumerate(zip((front_ref, kern_ref, gain_ref), small_out))
    ]
    for copy in copies:
        copy.start()
    for copy in copies + place_pieces(1, rec, down_ref, up_ref, stage, sems):
        copy.wait()


def place(own, rec):
    big = [jax.ShapeDtypeStruct((768, 1536), F32), jax.ShapeDtypeStruct((1536, 768), F32)]
    hbm = pl.BlockSpec(memory_space=pl.ANY)
    small = [(64, 1536), (5, 1536), (1536,)]
    scratch = [pltpu.VMEM((4, 8, 2, 48, 384), F32), pltpu.SemaphoreType.DMA((4, 8, 2))]
    started = pl.pallas_call(
        place_own_kernel,
        in_specs=[WHOLE] * 4,
        out_specs=[hbm] * 2,
        out_shape=big,
        scratch_shapes=scratch,
        compiler_params=vmem(40),
        cost_estimate=cost(1 << 20, 7 << 20),
    )(*own)
    return pl.pallas_call(
        place_rest_kernel,
        in_specs=[WHOLE] * 8 + [hbm] * 2,
        out_specs=[hbm] * 5,
        out_shape=big + [jax.ShapeDtypeStruct(shape, F32) for shape in small],
        input_output_aliases={8: 0, 9: 1},
        scratch_shapes=scratch
        + [pltpu.VMEM(shape, F32) for shape in small]
        + [pltpu.SemaphoreType.DMA((3,))],
        compiler_params=vmem(40),
        cost_estimate=cost(1 << 20, 7 << 20),
    )(*own, *rec, *started)


def high_low(value):
    high = value.astype(BF).astype(F32)
    return jnp.concatenate([high, value - high], axis=0).astype(BF)


def add_small(one, two):
    one, two = one.astype(F32), two.astype(F32)
    return high_low((one[:8] + one[8:]) + (two[:8] + two[8:]))


def tail_kernel(
    dln_ref, rec_ref, normed_ref, rstd_ref, frames_ref, segs_ref, stack_ref, cot_ref, kern_ref, gain_ref,
    keep_ref, send_ref, scaled, moved, sums,
):
    sums[...] = jnp.zeros_like(sums)
    taps = [kern_ref[pl.ds(j, 1), :] for j in range(5)]
    gain = gain_ref[...]
    wide_stack = stack_ref[...].astype(F32)
    for j in range(5):
        here = segs_ref[pl.ds(HALO, 128), :]
        same = (segs_ref[pl.ds(HALO - 2 + j, 128), :] == here).astype(F32)
        same = jnp.concatenate([same] * 4, axis=1)
        moved[pl.ds(128 * j, 128), :] = (same * wide_stack[HALO - 2 + j : HALO + 126 + j]).astype(BF)

    def fold(x):
        return x[0:8] + x[8:16]

    for r in range(0, 128, 16):
        at = pl.ds(r, 16)
        dln = dln_ref[at, :] + rec_ref[at, :].astype(F32)
        normed = normed_ref[at, :]
        rstd = rstd_ref[at, :][:, 0:1]
        sums[5] += fold(dln * normed)
        dnorm = dln * gain
        m1 = jnp.mean(dnorm, axis=1, keepdims=True)
        m2 = jnp.mean(dnorm * normed, axis=1, keepdims=True)
        dmixed = cot_ref[at, :].astype(F32) + rstd * (dnorm - m1 - normed * m2)
        dmixed = dmixed.astype(BF).astype(F32)
        here = segs_ref[pl.ds(HALO + r, 16), :]
        for j in range(5):
            near = frames_ref[pl.ds(HALO - 2 + r + j, 16), :]
            tap = taps[j]
            if j == 2:
                tap = tap + 1.0
                sums[j] += fold(dmixed * near)
            else:
                same = (segs_ref[pl.ds(HALO - 2 + r + j, 16), :] == here).astype(F32)
                same = jnp.concatenate([same] * 12, axis=1)
                sums[j] += fold(dmixed * (same * near))
            scaled[pl.ds(128 * j + r, 16), :] = (tap * dmixed).astype(BF)

    front = lax.dot_general(
        moved[...], scaled[...], (((0,), (0,)), ((), ())), preferred_element_type=F32
    )
    for d in range(4):
        keep_ref[pl.ds(64 * d, 64), :] = front[128 * d : 128 * d + 64]
        send_ref[pl.ds(64 * d, 64), :] = front[128 * d + 64 : 128 * d + 128].astype(BF)
    small = jnp.concatenate(
        [jnp.sum(sums[j], axis=0, keepdims=True) for j in range(6)] + [jnp.zeros((2, 1536), F32)], axis=0
    )
    small = high_low(small)
    keep_ref[pl.ds(256, 16), :] = small.astype(F32)
    send_ref[pl.ds(256, 16), :] = small


def tail(pieces, normed, rstd, frames, segs, stack, cot, kern, gain):
    args = (*pieces, normed, rstd, frames, segs, stack, cot, kern, gain)
    return pl.pallas_call(
        tail_kernel,
        in_specs=[WHOLE] * len(args),
        out_specs=[WHOLE] * 2,
        out_shape=[jax.ShapeDtypeStruct((272, 1536), F32), jax.ShapeDtypeStruct((272, 1536), BF)],
        scratch_shapes=[
            pltpu.VMEM((640, 1536), BF), pltpu.VMEM((640, 512), BF), pltpu.VMEM((6, 8, 1536), F32),
        ],
        compiler_params=vmem(16),
        cost_estimate=cost(60 * 10**9, 6 << 20),
    )(*args)


def gather_core(value):
    own = jnp.stack([value] + [xor_send(value, "tensor", m, 8) for m in ORDER[1:]])
    return own, xor_send(own, "tensor", 1, 8)


def after(value, *others):
    return lax.optimization_barrier((value, *others))[0]


def over(axis, value):
    return xor_send(value, *YZ[axis], 4)


def glue(kernel, outs, *args, flops=5 * 10**8):
    return pl.pallas_call(
        kernel,
        in_specs=[WHOLE] * len(args),
        out_specs=[WHOLE] * len(outs),
        out_shape=[jax.ShapeDtypeStruct(*out) for out in outs],
        compiler_params=vmem(16),
        cost_estimate=cost(flops, 1 << 16),
    )(*args)


def sum_kernel(one, two, three, four, out):
    out[...] = (one[...] + two[...]) + (three[...] + four[...])


def dln_core_kernel(own, rec, keep, send):
    for i in range(4):
        at, to = pl.ds(128 * i, 128), pl.ds(128 * (i // 2), 128)
        total = own[at, :].astype(F32) + rec[at, :].astype(F32)
        if i % 2:
            send[to, :] = total.astype(BF)
        else:
            keep[to, :] = total


def halve_kernel(own, rec, keep, send):
    n = keep.shape[0]
    keep[...] = own[pl.ds(0, n)] + rec[pl.ds(0, n)].astype(F32)
    send[...] = (own[pl.ds(n, n)] + rec[pl.ds(n, n)].astype(F32)).astype(BF)


def halve_first_kernel(own, rec, keep, send):
    n = keep.shape[0]
    keep[...] = own[pl.ds(0, n)].astype(F32) + rec[pl.ds(0, n)].astype(F32)
    send[...] = (own[pl.ds(n, n)].astype(F32) + rec[pl.ds(n, n)].astype(F32)).astype(BF)


def join_kernel(own0, rec0, own1, rec1, keep, send):
    for i, (own, rec) in enumerate(((own0, rec0), (own1, rec1))):
        total = own[...] + rec[...].astype(F32)
        keep[:, pl.ds(96 * i, 96), :] = total[:2]
        send[:, pl.ds(96 * i, 96), :] = total[2:].astype(BF)


def front_core_kernel(own, rec, keep0, keep1, send0, send1):
    for i in range(4):
        at = pl.ds(64 * i, 64)
        total = own[at, :] + rec[at, :].astype(F32)
        out = send0 if i % 2 else keep0
        out[pl.ds(64 * (i // 2), 64), :] = total[:, :768].astype(out.dtype)
        out = send1 if i // 2 else keep1
        out[pl.ds(64 * (i % 2), 64), :] = total[:, 768:].astype(out.dtype)
    small = add_small(own[pl.ds(256, 16), :], rec[pl.ds(256, 16), :])
    for i, (keep, send) in enumerate(((keep0, send0), (keep1, send1))):
        half = small[:, 768 * i : 768 * i + 768]
        keep[pl.ds(128, 16), :] = half.astype(F32)
        send[pl.ds(128, 16), :] = half


def front_x_kernel(own, rec, keep, send):
    keep[pl.ds(0, 64), :] = own[pl.ds(0, 64), :] + rec[pl.ds(0, 64), :].astype(F32)
    send[pl.ds(0, 64), :] = (own[pl.ds(64, 64), :] + rec[pl.ds(64, 64), :].astype(F32)).astype(BF)
    small = add_small(own[pl.ds(128, 16), :], rec[pl.ds(128, 16), :])
    keep[pl.ds(64, 16), :] = small.astype(F32)
    send[pl.ds(64, 16), :] = small


def spread_first_kernel(own, rec, front, front_rec, out0, out1):
    piece = (own[0] + rec[0].astype(F32)).astype(BF)
    front_rows = (front[pl.ds(0, 64), :] + front_rec[pl.ds(0, 64), :].astype(F32)).astype(BF)
    small = add_small(front[pl.ds(64, 16), :], front_rec[pl.ds(64, 16), :])
    for i, out in enumerate((out0, out1)):
        out[pl.ds(0, 96), :] = piece[96 * i : 96 * i + 96]
        cols = slice(384 * i, 384 * i + 384)
        out[pl.ds(96, 64), :] = front_rows[:, cols]
        out[pl.ds(160, 16), :] = small[:, cols]


def spread_kernel(own, rec, out):
    n = own.shape[0] - 80
    out[pl.ds(0, n), :] = own[pl.ds(0, n), :]
    out[pl.ds(n, n), :] = rec[pl.ds(0, n), :]
    out[pl.ds(2 * n, 64), :] = (own[pl.ds(n, 64), :].astype(F32) + rec[pl.ds(n, 64), :].astype(F32)).astype(BF)
    out[pl.ds(2 * n + 64, 16), :] = add_small(own[pl.ds(n + 64, 16), :], rec[pl.ds(n + 64, 16), :])


def halve_first(keep, rec):
    return glue(halve_first_kernel, [((4, 96, 384), F32), ((4, 96, 384), BF)], keep, rec)


def join_parts(k, pairs, recs):
    return glue(
        join_kernel, [((2, 192, 384), F32), ((2, 192, 384), BF)],
        pairs[k][0], recs[0], pairs[k + 1][0], recs[1],
    )


def reduce_ends(k, keep, send):
    keep, send = glue(
        halve_kernel, [((1, 192, 384), F32), ((1, 192, 384), BF)], keep, over(PARTS[k][2], send)
    )
    return keep, over(PARTS[k][3], send)


def spread_parts(ends, fronts):
    bufs = []
    for k in (0, 1):
        bufs += glue(spread_first_kernel, [((176, 384), BF)] * 2, *ends[k], *fronts[k])
    for s in (3, 2, 1):
        recs = [over(SPREAD[k][s], bufs[k]) for k in range(4)]
        rows = 2 * bufs[0].shape[0] - 80
        bufs = [glue(spread_kernel, [((rows, 384), BF)], bufs[k], recs[k])[0] for k in range(4)]
    return bufs, [over(SPREAD[k][0], bufs[k]) for k in range(4)]


def per_device(
    panels, lengths, segments, front_weight, conv_kernel, gain, up_weight, down_weight, cotangent
):
    gain_row = gain[None, :]
    cot = cotangent[0]

    picked = select_panels(lengths, jnp.transpose(panels[0, 0], (1, 2, 0)), segments)
    front_weight = after(front_weight, picked[0])
    got = [xor_send(picked[e], "context", e, 4) for e in (2, 1, 3)]
    wa, wb = gather_core(front_weight)
    (block,) = glue(sum_kernel, [((640, 128), BF)], picked[0], *got)
    cot_later = after(cot, block)
    pa, pb = gather_core(block)
    others = [xor_send(cot_later, "tensor", m ^ 1, 8) for m in ORDER]

    ln, normed, rstd, frames, segs, stack = normalise(pa, pb, wa, wb, conv_kernel, gain_row)
    hidden, slope, ln_t = hidden_rows(ln, up_weight, down_weight)
    slope, *others = lax.optimization_barrier((slope, *others))
    cb = jnp.stack(others)
    ca = xor_send(cb, "tensor", 1, 8)
    dpre_a, dln_keep = backward_rows(0, ca, slope, up_weight, down_weight)
    dpre_b, dln_send = backward_rows(1, cb, slope, up_weight, down_weight)

    dln_rec = xor_send(dln_send, "tensor", 1, 8)
    keep, send = glue(
        dln_core_kernel, [((256, 1536), F32), ((256, 1536), BF)], dln_keep, dln_rec
    )
    rec = xor_send(send, "tensor", 2, 8)
    parts = [weight_part(k, hidden, ca, cb, ln_t, dpre_a, dpre_b) for k in range(4)]
    firsts = [over(PARTS[k][0], parts[k][1]) for k in range(4)]
    pairs = [halve_first(parts[0][0], firsts[0])]
    rec = after(rec, pairs[0][1], *[p[0] for p in parts[1:]])
    keep, send = glue(halve_kernel, [((128, 1536), F32), ((128, 1536), BF)], keep, rec)
    pairs.append(halve_first(parts[1][0], firsts[1]))
    send = after(send, pairs[1][1])
    rec = xor_send(send, "tensor", 6, 8)
    pairs += [halve_first(parts[k][0], firsts[k]) for k in (2, 3)]
    seconds = [over(PARTS[k][1], pairs[k][1]) for k in range(4)]
    joined = join_parts(0, pairs, seconds[:2])
    pieces = (keep, after(rec, joined[1], *seconds[2:]))
    keep, send = tail(pieces, normed, rstd, frames, segs, stack, cot, conv_kernel, gain_row)
    ends = reduce_ends(0, *joined), reduce_ends(2, *join_parts(2, pairs, seconds[2:]))
    k0, k1, s0, s1 = glue(
        front_core_kernel, [((144, 768), F32)] * 2 + [((144, 768), BF)] * 2,
        keep, xor_send(send, "tensor", 1, 8), flops=FIRST,
    )
    half = [((80, 768), F32), ((80, 768), BF)]
    k0, s0 = glue(front_x_kernel, half, k0, xor_send(s0, "tensor", 2, 8), flops=FIRST)
    k1, s1 = glue(front_x_kernel, half, k1, xor_send(s1, "tensor", 6, 8), flops=FIRST)
    fronts = (k0, xor_send(s0, "tensor", 6, 8)), (k1, xor_send(s1, "tensor", 2, 8))
    own, rec = spread_parts(ends, fronts)
    grad_down, grad_up, grad_front, grad_kernel, grad_gain = place(own, rec)
    return (grad_front, grad_kernel, grad_gain, grad_up, grad_down)


def solution(mesh):
    return jax.shard_map(
        per_device,
        mesh=mesh,
        in_specs=(
            P("dp", "context", None, None, "tensor"),
            P("dp", None),
            P("dp", ("context", "tensor")),
            P("tensor", None),
            P(),
            P(),
            P(None, "tensor"),
            P("tensor", None),
            P("dp", ("context", "tensor"), None),
        ),
        out_specs=(P("tensor", None), P(), P(), P(None, "tensor"), P("tensor", None)),
        check_vma=False,
    )
```
